32 devices in a mesh: gx: 4 (over y, x), gy: 2 (over core), gz: 4 (over z).
Axes of the slice: x: 2, y: 2, z: 4, core: 2. Of those that a mesh axis runs over, the one named last changes fastest.
Arguments:
- frac: float32 [3, 4, 2, 8, 128], P(None, 'gx', 'gy', 'gz'), may hold values from 0 to 1
- velocity: float32 [3, 4, 2, 8, 128], P(None, 'gx', 'gy', 'gz'), may hold values from -2 to 2
- force_old: float32 [3, 4, 2, 8, 128], P(None, 'gx', 'gy', 'gz'), may hold values from -6 to 6
- species: int32 [4, 2, 8, 128], P('gx', 'gy', 'gz'), may hold values from 0 to 9
- cell_count: int32 [4, 2, 8], P('gx', 'gy', 'gz'), may hold values from 1 to 128, as said below
- neighbours: int32 [16, 4, 2, 8, 128], P(None, 'gx', 'gy', 'gz'), may hold values from 0 to 3455, as said below
- embed: bfloat16 [10, 64], replicated, may hold values from -6 to 6
- w_radial_in: bfloat16 [8, 64], replicated, may hold values from -2 to 2
- w_radial_out: bfloat16 [64, 192], replicated, may hold values from -0.75 to 0.75
- w_node: bfloat16 [256, 64], replicated, may hold values from -0.375 to 0.375
- w_energy: float32 [64], replicated, may hold values from -0.75 to 0.75
Outputs:
- next_frac: float32 [3, 4, 2, 8, 128], P(None, 'gx', 'gy', 'gz')
- next_velocity: float32 [3, 4, 2, 8, 128], P(None, 'gx', 'gy', 'gz')
- next_force: float32 [3, 4, 2, 8, 128], P(None, 'gx', 'gy', 'gz')
- site_energy: float32 [4, 2, 8, 128], P('gx', 'gy', 'gz')
The draws below stay inside these ranges and needn't reach their ends.
Inputs may be any that keep to these rules, and one draw needn't show every extreme that they name: `cell_count`: in every draw at least one cell holds exactly 128 atoms; the other cells hold 1 to 128. `neighbours`: each code o * 128 + s names slot s of the cell at offset (o // 9 - 1, (o // 3) % 3 - 1, o % 3 - 1) from the receiver's cell, periodic; s is below that cell's count; no code names the receiver itself.
All inputs are finite; a program needn't handle non-finite values.
Results may differ from the reference program's by a relative error of at most 0.015.
Values may be sent and summed in bfloat16 or wider, within the bound.
A program may use at most 64 MiB of HBM per device.

```python
import math
import jax
import jax.numpy as jnp
import numpy as np
from jax import lax

CH = 64
NB = 8
NSPEC = 10
K = 16
CAP = 128
NX = 4
NY = 2
NZ = 8


def count_field(key):
    key_a, key_b, key_c, key_d = jax.random.split(key, 4)
    first = jax.random.randint(key_a, (NX, NY, NZ), 1, CAP + 1)
    second = jax.random.randint(key_b, (NX, NY, NZ), 1, CAP + 1)
    base = 1 + first * second // CAP
    centre = jax.random.randint(key_c, (3,), 0, 1 << 20)
    grid_a = jnp.arange(NX, dtype=jnp.int32)[:, None, None]
    grid_b = jnp.arange(NY, dtype=jnp.int32)[None, :, None]
    grid_c = jnp.arange(NZ, dtype=jnp.int32)[None, None, :]
    dist_a = (grid_a - centre[0] % NX) % NX
    dist_b = (grid_b - centre[1] % NY) % NY
    dist_c = (grid_c - centre[2] % NZ) % NZ
    inside_a = jnp.minimum(dist_a, NX - dist_a) < max(NX // 4, 1)
    inside_b = jnp.minimum(dist_b, NY - dist_b) < max(NY // 4, 1)
    inside_c = jnp.minimum(dist_c, NZ - dist_c) < max(NZ // 4, 1)
    dense = inside_a & inside_b & inside_c
    counts = jnp.minimum(jnp.where(dense, 3 * base, base), CAP)
    chosen = jax.random.randint(key_d, (), 0, NX * NY * NZ)
    counts = counts.reshape(-1).at[chosen].set(CAP).reshape(NX, NY, NZ)
    return counts.astype(jnp.int32)


def draw_cell_count(key, part):
    return count_field(jax.random.fold_in(key, 7))


def draw_neighbours(key, part):
    counts = count_field(jax.random.fold_in(key, 7))
    key_a, key_b, key_c = jax.random.split(jax.random.fold_in(key, 8), 3)
    shape = (K, NX, NY, NZ, CAP)
    nearby = jax.random.randint(key_a, shape, 0, 2)
    spread = jax.random.randint(key_b, shape, 0, 27)
    offset = jnp.where(nearby == 0, 13, spread)
    grid_a = jnp.arange(NX, dtype=jnp.int32)[None, :, None, None, None]
    grid_b = jnp.arange(NY, dtype=jnp.int32)[None, None, :, None, None]
    grid_c = jnp.arange(NZ, dtype=jnp.int32)[None, None, None, :, None]
    slot_grid = jnp.arange(CAP, dtype=jnp.int32)[None, None, None, None, :]
    target = counts[(grid_a + offset // 9 - 1) % NX, (grid_b + offset // 3 % 3 - 1) % NY, (grid_c + offset % 3 - 1) % NZ]
    picked = jax.random.randint(key_c, shape, 0, 65536)
    slot_id = picked * target // 65536
    itself = (offset == 13) & (slot_id == slot_grid)
    offset = jnp.where(itself, 14, offset)
    slot_id = jnp.where(itself, 0, slot_id)
    return (offset * CAP + slot_id).astype(jnp.int32)


def set_ends(values, own_key, smallest, high):
    longest = values.shape.index(max(values.shape))
    spots = []
    for shift in (0, 1):
        where = [jax.random.randint(jax.random.fold_in(own_key, axis), (), 0, length) for axis, length in enumerate(values.shape)]
        where[longest] = (where[longest] + shift) % values.shape[longest]
        spots.append(tuple(where))
    return values.at[spots[0]].set(smallest).at[spots[1]].set(high)


def block_levels(key, shape, pieces, least, top_value):
    def one(axis_at, parts):
        heights = jax.random.uniform(jax.random.fold_in(jax.random.fold_in(key, 6), axis_at), (parts,), jnp.float32, least / len(pieces), top_value / len(pieces))
        return jnp.repeat(jnp.exp(heights), shape[axis_at] // parts).reshape((-1,) + (1,) * (len(shape) - axis_at - 1))

    loudness = one(*pieces[0])
    for cut in pieces[1:]:
        loudness = loudness * one(*cut)
    return loudness


def cumulative_ranks(amount, slope):
    loads = [(1 << 20) // math.isqrt(rank ** slope) + 1 for rank in range(1, amount + 1)]
    scale = 1 + sum(loads) // (1 << 30)
    return np.cumsum(np.array([max(1, weight // scale) for weight in loads]))


def skewed_ids(stream_key, extent, count, skew):
    table = cumulative_ranks(count, skew)
    pick = jax.random.randint(jax.random.fold_in(stream_key, 1), extent, 0, int(table[count - 1]))
    grade = jnp.searchsorted(jnp.asarray(table, jnp.int32), pick, side="right")
    return jax.random.permutation(jax.random.fold_in(stream_key, 2), count)[grade].astype(jnp.int32)


def gaussian(own_key, extent, deviation, bound, cuts=(), held_as=jnp.bfloat16):
    gain = block_levels(own_key, extent, cuts, -0.22, 0.18) if cuts else 1.0
    entries = jax.random.normal(own_key, extent, jnp.float32) * deviation * gain
    return jnp.minimum(jnp.maximum(entries, -bound), bound).astype(held_as)


def setup_inputs(seed: int = 0) -> dict:
    seeds = jax.random.split(jax.random.key(seed), 12)
    frac = jnp.clip(1.0 * jax.random.uniform(seeds[0], (3, NX, NY, NZ, CAP), jnp.float32) ** block_levels(seeds[0], (3, NX, NY, NZ, CAP), ((1, 4), (2, 2), (3, 4)), -0.2, 0.2), 0.0, 1.0)
    velocity = gaussian(seeds[1], (3, NX, NY, NZ, CAP), 0.3, 2.0, ((1, 4), (2, 2), (3, 4)), jnp.float32)
    force_old = gaussian(seeds[2], (3, NX, NY, NZ, CAP), 1.0, 6.0, ((1, 4), (2, 2), (3, 4)), jnp.float32)
    species = set_ends(skewed_ids(seeds[3], (NX, NY, NZ, CAP), NSPEC, 2), jax.random.fold_in(seeds[3], 3), 0, NSPEC - 1).astype(jnp.int32)
    cell_count = draw_cell_count(jax.random.fold_in(seeds[11], 71), 0)
    neighbours = draw_neighbours(jax.random.fold_in(seeds[11], 71), 0)
    embed = gaussian(seeds[6], (NSPEC, CH), 1.0, 6.0)
    w_radial_in = gaussian(seeds[7], (NB, CH), NB ** -0.5, 2.0)
    w_radial_out = gaussian(seeds[8], (CH, 3 * CH), CH ** -0.5, 0.75)
    w_node = gaussian(seeds[9], (4 * CH, CH), (4 * CH) ** -0.5, 0.375)
    w_energy = gaussian(seeds[10], (CH,), CH ** -0.5, 0.75, (), jnp.float32)
    return {"frac": frac, "velocity": velocity, "force_old": force_old, "species": species, "cell_count": cell_count, "neighbours": neighbours, "embed": embed, "w_radial_in": w_radial_in, "w_radial_out": w_radial_out, "w_node": w_node, "w_energy": w_energy}


MASSES = (1.008, 12.011, 14.007, 15.999, 32.06, 22.99, 35.45, 39.098, 24.305, 40.078)
SQRT3 = 1.7320508075688772
HALF_SQRT3 = 0.8660254037844386
TIME_STEP = 0.5

def species_mass(species):
    table = jnp.asarray(MASSES, dtype=jnp.float32) / 16.0
    shape_ones = (1,) * species.ndim
    which = species[None] == jnp.arange(len(MASSES), dtype=jnp.int32).reshape((-1,) + shape_ones)
    return lax.optimization_barrier(jnp.sum(jnp.where(which, table.reshape((-1,) + shape_ones), 0.0), axis=0))

def embed_species(species_flat, embed):
    kinds = embed.shape[0]
    onehot = (species_flat[None, :] == jnp.arange(kinds, dtype=jnp.int32)[:, None]).astype(jnp.bfloat16)
    return jnp.dot(embed.T, onehot, preferred_element_type=jnp.float32).astype(jnp.bfloat16)

def site_terms(displace, send_feat, own_feat, w_radial_in, w_radial_out, w_node, w_energy):
    basis_count = w_radial_in.shape[0]
    channels = own_feat.shape[0]
    candidates = displace.shape[1]
    block_size = displace.shape[2]
    squared = lax.optimization_barrier(jnp.sum(displace * displace, axis=0))
    envelope = jnp.maximum(1.0 - squared, 0.0) ** 3
    centres = jnp.arange(basis_count, dtype=jnp.float32) / (basis_count - 1)
    basis_values = jnp.exp(-float((basis_count - 1) ** 2) * (squared[None] - centres[:, None, None]) ** 2)
    basis_values = basis_values.astype(jnp.bfloat16).reshape(basis_count, candidates * block_size)
    hidden = jax.nn.silu(jnp.dot(w_radial_in.T, basis_values, preferred_element_type=jnp.float32)).astype(jnp.bfloat16)
    radial = jnp.dot(w_radial_out.T, hidden, preferred_element_type=jnp.float32)
    radial = radial.reshape(3, channels, candidates, block_size) * envelope[None, None]
    along_x = displace[0]
    along_y = displace[1]
    along_z = displace[2]
    first_order = jnp.stack([along_x, along_y, along_z])
    second_order = jnp.stack([SQRT3 * along_x * along_y, SQRT3 * along_y * along_z, SQRT3 * along_z * along_x, HALF_SQRT3 * (along_x * along_x - along_y * along_y), 0.5 * (2.0 * along_z * along_z - along_x * along_x - along_y * along_y)])
    carried = radial * send_feat.astype(jnp.float32)[None]
    scalar_part = lax.optimization_barrier(jnp.sum(carried[0], axis=1))
    vector_part = lax.optimization_barrier(jnp.sum(carried[1][None] * first_order[:, None], axis=2))
    tensor_part = lax.optimization_barrier(jnp.sum(carried[2][None] * second_order[:, None], axis=2))
    invariant = jnp.concatenate([scalar_part, lax.optimization_barrier(jnp.sum(vector_part * vector_part, axis=0)), lax.optimization_barrier(jnp.sum(tensor_part * tensor_part, axis=0)), own_feat.astype(jnp.float32)], axis=0).astype(jnp.bfloat16)
    activity = jax.nn.silu(jnp.dot(w_node.T, invariant, preferred_element_type=jnp.float32))
    return lax.optimization_barrier(jnp.sum(w_energy[:, None] * activity, axis=0))

def reference(frac, velocity, force_old, species, cell_count, neighbours, embed, w_radial_in, w_radial_out, w_node, w_energy):
    cells_x, cells_y, cells_z, capacity = species.shape
    candidates = neighbours.shape[0]
    total = cells_x * cells_y * cells_z * capacity
    block_size = 16 * capacity
    occupied = (lax.broadcasted_iota(jnp.int32, species.shape, 3) < cell_count[..., None]).astype(jnp.float32)
    atom_mass = species_mass(species)
    half_velocity = velocity + 0.5 * TIME_STEP * force_old / atom_mass
    moved = frac + TIME_STEP * half_velocity
    feats = embed_species(species.reshape(total), embed)
    moved_flat = moved.reshape(3, total)
    codes = neighbours.reshape(candidates, total)
    occupied_flat = occupied.reshape(total)

    def one_block(carried, number):
        forces, energies = carried
        start = number * block_size
        receivers = start + jnp.arange(block_size, dtype=jnp.int32)
        cell_id = receivers // capacity
        cell_a = cell_id // (cells_y * cells_z)
        cell_b = cell_id // cells_z % cells_y
        cell_c = cell_id % cells_z
        packed = lax.dynamic_slice_in_dim(codes, start, block_size, 1)
        offset = packed // capacity
        slot_id = packed % capacity
        shift_a = offset // 9 - 1
        shift_b = offset // 3 % 3 - 1
        shift_c = offset % 3 - 1
        senders = (((cell_a + shift_a) % cells_x * cells_y + (cell_b + shift_b) % cells_y) * cells_z + (cell_c + shift_c) % cells_z) * capacity + slot_id
        cell_shift = jnp.stack([shift_a, shift_b, shift_c]).astype(jnp.float32)
        own_pos = lax.dynamic_slice_in_dim(moved_flat, start, block_size, 1)
        displace = cell_shift + moved_flat[:, senders] - own_pos[:, None, :]
        send_feat = feats[:, senders]
        own_feat = lax.dynamic_slice_in_dim(feats, start, block_size, 1)
        weights = lax.dynamic_slice_in_dim(occupied_flat, start, block_size, 0)

        def energy_of(shifted):
            return site_terms(shifted, send_feat, own_feat, w_radial_in, w_radial_out, w_node, w_energy)
        energy, pullback = jax.vjp(energy_of, displace)
        gradient = pullback(weights)[0]
        forces = forces.at[:, receivers].add(lax.optimization_barrier(jnp.sum(gradient, axis=1)))
        forces = forces.at[:, senders.reshape(-1)].add(-gradient.reshape(3, -1))
        energies = lax.dynamic_update_slice_in_dim(energies, energy, start, 0)
        return ((forces, energies), None)
    start_state = (jnp.zeros((3, total), jnp.float32), jnp.zeros((total,), jnp.float32))
    blocks = jnp.arange(total // block_size, dtype=jnp.int32)
    (forces, energies), _ = lax.scan(one_block, start_state, blocks)
    next_force = occupied * forces.reshape(3, cells_x, cells_y, cells_z, capacity)
    next_velocity = occupied * (half_velocity + 0.5 * TIME_STEP * next_force / atom_mass)
    next_frac = occupied * moved
    site_energy = occupied * energies.reshape(cells_x, cells_y, cells_z, capacity)
    return (next_frac, next_velocity, next_force, site_energy)
```

```python
import functools
import itertools

import jax
import jax.numpy as jnp
from jax import lax
from jax.experimental import pallas as pl
from jax.experimental.pallas import tpu as pltpu
from jax.sharding import PartitionSpec as P

MASSES = (1.008, 12.011, 14.007, 15.999, 32.06, 22.99, 35.45, 39.098, 24.305, 40.078)
SQRT3 = 1.7320508075688772
HALF_SQRT3 = 0.8660254037844386
TIME_STEP = 0.5
AXES = ("gx", "gy", "gz")
MESH = pl.DeviceIdType.MESH
F32 = jnp.float32
BF16 = jnp.bfloat16
CHUNK = 4
INPUTS = 11


def canonical(coordinate, cells, total):
    return coordinate % total if total < cells + 2 else coordinate


def halo_plan(cells, sizes):
    totals = [c * s for c, s in zip(cells, sizes)]
    spans = [sorted({canonical(e, c, t) for e in range(-1, c + 1)}) for c, t in zip(cells, totals)]
    plan = []
    for at in itertools.product(*spans):
        step = tuple(e // c for e, c in zip(at, cells))
        inner = tuple(e % c for e, c in zip(at, cells))
        plan.append((at, step, inner))
    return spans, totals, plan


def dot(a, b, ca=1, cb=0):
    return lax.dot_general(a, b, (((ca,), (cb,)), ((), ())), preferred_element_type=F32)


def silu_parts(pre):
    sig = 0.5 * jnp.tanh(0.5 * pre) + 0.5
    return pre * sig, sig * (1.0 + pre * (1.0 - sig))


def harmonics(x, y, z):
    return (
        None,
        x,
        y,
        z,
        SQRT3 * x * y,
        SQRT3 * y * z,
        SQRT3 * z * x,
        HALF_SQRT3 * (x * x - y * y),
        0.5 * (2.0 * z * z - x * x - y * y),
    )


DEGREE = (0, 1, 1, 1, 2, 2, 2, 2, 2)
COUNT = len(DEGREE)


def message_groups(plan, index_of, sizes):
    moves = [(i, step, index_of[inner]) for i, (_, step, inner) in enumerate(plan)]
    runs = []
    for i, step, own in moves:
        if not any(s % n for s, n in zip(step, sizes)):
            continue
        last = runs[-1] if runs else None
        if last and last[0] == step and last[1] + last[3] == i and last[2] + last[3] == own:
            runs[-1] = (step, last[1], last[2], last[3] + 1)
        else:
            runs.append((step, i, own, 1))
    return runs


def step_kernel(sizes, *refs):
    count = refs[3].shape[0] * refs[3].shape[1] * refs[3].shape[2]
    cap, cand, chan = refs[3].shape[3], refs[5].shape[0], refs[6].shape[1]
    spread_rows = refs[INPUTS + 4 + INPUTS + 1].shape[0] * 4
    spread_rows = -(-spread_rows // 16) * 16
    pair_rows = count * cand
    pl.run_scoped(
        functools.partial(step_body, sizes, refs),
        pltpu.VMEM((pair_rows, cap, cap), BF16),
        pltpu.VMEM((pair_rows, spread_rows, cap), BF16),
        pltpu.VMEM((pair_rows, 3 * chan, cap), BF16),
        pltpu.VMEM((pair_rows, chan, cap), BF16),
        pltpu.VMEM((pair_rows, chan, cap), BF16),
        pltpu.VMEM((pair_rows, 16 * COUNT, cap), BF16),
        pltpu.VMEM((count, COUNT, chan, cap), BF16),
    )


def step_body(sizes, refs, onehot, chosen, prod, feat_s, slope, wts, grad_s):
    sources, outs, held = refs[:INPUTS], refs[INPUTS : INPUTS + 4], refs[INPUTS + 4 :]
    next_frac, next_velocity, next_force, site_energy = outs
    staged, held = held[:INPUTS], held[INPUTS:]
    frac, velocity, force_old, species, cell_count, neighbours, embed, w_in, w_out, w_node_t, w_energy = staged
    table, back, landed, edge_s, ysc, gsc, rows_s, ints_s, msg_s, embed_t = held[:10]
    send_a, recv_a, send_b, recv_b, load_sem = held[10:]
    cells = species.shape[:3]
    cap = species.shape[3]
    cand = neighbours.shape[0]
    chan = embed.shape[1]
    kinds = embed.shape[0]
    nb = w_in.shape[0]
    spans, totals, plan = halo_plan(cells, sizes)
    index_of = {at: i for i, (at, _, _) in enumerate(plan)}
    inner_cells = list(itertools.product(*[range(c) for c in cells]))
    me = [lax.axis_index(a) for a in AXES]

    def device(step):
        return {
            a: lax.rem(m + s + n, n) for a, m, s, n in zip(AXES, me, step, sizes)
        }

    runs = message_groups(plan, index_of, sizes)
    runs = sorted(runs, key=lambda r: (r[0][2] == 0, r[0][0] == 0))
    others = sorted({tuple(s % n for s, n in zip(step, sizes)) for step, _, _, _ in runs})
    barrier = pltpu.get_barrier_semaphore()
    for step in others:
        pl.semaphore_signal(barrier, inc=1, device_id=device(step), device_id_type=MESH)
    loads = [pltpu.make_async_copy(sources[i], staged[i], load_sem.at[i]) for i in range(INPUTS)]
    for load in loads:
        load.start()
    for load in loads[:5]:
        load.wait()

    rows = {}
    for c, (a, b, z) in enumerate(inner_cells):
        kind = species[a, b, pl.ds(z, 1), :]
        mass = jnp.zeros((1, cap), F32)
        for n, value in enumerate(MASSES):
            mass = jnp.where(kind == n, value / 16.0, mass)
        lane = lax.broadcasted_iota(jnp.int32, (1, cap), 1)
        occ = (lane < cell_count[a, b, z]).astype(F32)
        e = index_of[(a, b, z)]
        moved, half = [], []
        for d in range(3):
            h = velocity[d, a, b, pl.ds(z, 1), :] + 0.5 * TIME_STEP * force_old[d, a, b, pl.ds(z, 1), :] / mass
            m = frac[d, a, b, pl.ds(z, 1), :] + TIME_STEP * h
            table[e, d : d + 1, :] = m
            next_frac[d, a, b, pl.ds(z, 1), :] = occ * m
            half.append(h)
            moved.append(m)
        table[e, 3:4, :] = kind.astype(F32)
        rows[c] = (kind, mass, occ, moved, half)

    pl.semaphore_wait(barrier, len(others))
    copies = []
    for n, (step, there, own, length) in enumerate(runs):
        copy = pltpu.make_async_remote_copy(
            src_ref=table.at[pl.ds(own, length)],
            dst_ref=table.at[pl.ds(there, length)],
            send_sem=send_a.at[n],
            recv_sem=recv_a.at[n],
            device_id=device(tuple(-s for s in step)),
            device_id_type=MESH,
        )
        copy.start()
        copies.append(copy)

    for load in loads[5:]:
        load.wait()
    shift_bits = cap.bit_length() - 1
    pairs = {}
    slot_lanes = lax.broadcasted_iota(jnp.int32, (cap, cap), 1)
    tiles = chosen.shape[1] // 16
    quarter = lax.broadcasted_iota(jnp.int32, (16, cap), 0) >> 2
    for c, (a, b, z) in enumerate(inner_cells):
        at = pl.ds(c * cand, cand)
        for k in range(cand):
            ints_s[0, pl.ds(c * cand + k, 1), :] = neighbours[k, a, b, pl.ds(z, 1), :]
        code = ints_s[0, at, :]
        if cap == 1 << shift_bits:
            offset, slot = code >> shift_bits, code & (cap - 1)
        else:
            offset, slot = code // cap, code % cap
        third = (offset * 43) >> 7
        ninth = (offset * 57) >> 9
        shifts = (ninth - 1, third - 3 * ninth - 1, offset - 3 * third - 1)
        cell = jnp.zeros_like(code)
        for axis in range(3):
            place = (a, b, z)[axis] + shifts[axis]
            low = spans[axis][0]
            if totals[axis] < cells[axis] + 2:
                place = jnp.where(place < 0, place + totals[axis], place)
                place = jnp.where(place >= totals[axis], place - totals[axis], place)
            cell = cell * len(spans[axis]) + (place - low)
        ints_s[2, at, :] = cell
        pairs[c] = (slot, cell, [s.astype(F32) for s in shifts])
        slot_columns = slot.T
        for k in range(cand):
            hit = jnp.broadcast_to(slot_columns[:, k : k + 1], (cap, cap)) == slot_lanes
            onehot[c * cand + k] = jnp.where(hit, 1.0, 0.0).astype(BF16)
            where = jnp.broadcast_to(ints_s[2, pl.ds(c * cand + k, 1), :], (16, cap)) - quarter
            for t in range(tiles):
                chosen[c * cand + k, 16 * t : 16 * t + 16, :] = jnp.where(where == 4 * t, 1.0, 0.0).astype(BF16)

    w_in_half = (0.5 * w_in[...].astype(F32)).astype(BF16)
    w_in_t = (0.5 * w_in[...].astype(F32)).T.astype(BF16)
    w_out_t = w_out[...].astype(F32).T.astype(BF16)
    diag = lax.broadcasted_iota(jnp.int32, (chan, chan), 0) == lax.broadcasted_iota(jnp.int32, (chan, chan), 1)
    energy_row = jnp.broadcast_to(w_energy[...], (chan, chan))
    energy_col = jnp.sum(jnp.where(diag, energy_row, 0.0), axis=1, keepdims=True)
    kind_rows = lax.broadcasted_iota(jnp.int32, (kinds, cap), 0)
    centres = lax.broadcasted_iota(jnp.int32, (nb, cap), 0).astype(F32) / (nb - 1)
    kind_lanes = lax.broadcasted_iota(jnp.int32, (kinds, cap), 1)
    embed_t[...] = dot(embed[...], (kind_rows == kind_lanes).astype(F32).astype(BF16), 0, 0)
    own_feat = {
        c: dot(embed[...], (kind_rows == rows[c][0]).astype(F32).astype(BF16), 0, 0).astype(BF16)
        for c in rows
    }
    adders = jnp.where(
        lax.broadcasted_iota(jnp.int32, (16, COUNT * 16), 1) // 16
        == lax.broadcasted_iota(jnp.int32, (16, COUNT * 16), 0),
        1.0,
        0.0,
    ).astype(BF16)

    near = {
        c: {
            index_of[tuple(canonical(p + s, n, t) for p, s, n, t in zip(at, move, cells, totals))]
            for move in itertools.product((-1, 0, 1), repeat=3)
        }
        for c, at in enumerate(inner_cells)
    }
    found = {c: [jnp.zeros((cand, cap), F32) for _ in range(4)] for c in near}

    def take(cells_here):
        for e in cells_here:
            for c in near:
                if e in near[c]:
                    slot, cell, _ = pairs[c]
                    hit = cell == e
                    for q in range(4):
                        row = jnp.broadcast_to(table[e, q : q + 1, :], (cand, cap))
                        found[c][q] = jnp.where(hit, jnp.take_along_axis(row, slot, axis=1), found[c][q])

    arriving = {there + j for _, there, _, length in runs for j in range(length)}
    take([i for i in range(len(plan)) if i not in arriving])
    for flat in (True, False):
        group = [n for n, r in enumerate(runs) if (r[0][2] == 0) == flat]
        for n in group:
            copies[n].wait_recv()
        take([runs[n][1] + j for n in group for j in range(runs[n][3])])

    geometry = {}
    for c in near:
        slot, cell, shifts = pairs[c]
        x, y, w = [s + f - m for s, f, m in zip(shifts, found[c], rows[c][3])]
        squared = x * x + y * y + w * w
        rest = jnp.maximum(1.0 - squared, 0.0)
        envelope = rest * rest * rest
        geometry[c] = (x, y, w, squared, rest, envelope)
        at = pl.ds(c * cand, cand)
        rows_s[0, at, :] = squared
        ints_s[0, at, :] = found[c][3].astype(jnp.int32)
        for m, value in enumerate(harmonics(x, y, w)):
            ysc[m, at, :] = envelope if value is None else value * envelope

    sharp = float((nb - 1) ** 2)

    def forward(c, g):
        first = c * cand + g * CHUNK
        basis = []
        for k in range(CHUNK):
            gap = rows_s[0, pl.ds(first + k, 1), :] - centres
            value = jnp.exp(-sharp * (gap * gap))
            edge_s[first + k] = value * gap
            basis.append(value.astype(BF16))
        half = dot(w_in_t, jnp.concatenate(basis, axis=1))
        t = jnp.tanh(half)
        up = 1.0 + t
        hidden = half * up
        tilt = (up + hidden * (1.0 - t)).astype(BF16)
        for k in range(CHUNK):
            slope[first + k] = tilt[:, k * cap : (k + 1) * cap]
        radial = dot(w_out_t, hidden.astype(BF16)).astype(BF16)
        weight = []
        for k in range(CHUNK):
            row = []
            for m in range(COUNT):
                value = jnp.broadcast_to(ysc[m, pl.ds(first + k, 1), :], (16, cap)).astype(BF16)
                wts[first + k, 16 * m : 16 * m + 16, :] = value
                row.append(value)
            weight.append(row)
        for s in range(chan // 16):
            top = 16 * s
            carried = [[], [], []]
            for k in range(CHUNK):
                kind = jnp.broadcast_to(ints_s[0, pl.ds(first + k, 1), :], (16, cap))
                feat = jnp.take_along_axis(embed_t[top : top + 16, :], kind, axis=1).astype(BF16)
                feat_s[first + k, top : top + 16, :] = feat
                for d in range(3):
                    value = radial[d * chan + top : d * chan + top + 16, k * cap : (k + 1) * cap] * feat
                    prod[first + k, d * chan + top : d * chan + top + 16, :] = value
                    carried[d].append(value)
            for m in range(COUNT):
                terms = [carried[DEGREE[m]][k] * weight[k][m] for k in range(CHUNK)]
                while len(terms) > 1:
                    terms = [p + q for p, q in zip(terms[::2], terms[1::2])]
                total = terms[0].astype(F32)
                msg_s[c, m, top : top + 16, :] = total if g == 0 else msg_s[c, m, top : top + 16, :] + total

    def node(c):
        occ = rows[c][2]
        msg = [msg_s[c, m] for m in range(COUNT)]
        vector = msg[1] * msg[1] + msg[2] * msg[2] + msg[3] * msg[3]
        tensor = msg[4] * msg[4]
        for m in range(5, 9):
            tensor = tensor + msg[m] * msg[m]
        invariant = jnp.concatenate([msg[0].astype(BF16), vector.astype(BF16), tensor.astype(BF16), own_feat[c]], axis=0)
        active, tilt = silu_parts(dot(w_node_t[...], invariant))
        d_pre = (energy_col * occ * tilt).astype(BF16)
        d_inv = dot(w_node_t[:, 0 : 3 * chan], d_pre, 0, 0).astype(BF16).astype(F32)
        grad_s[c, 0] = d_inv[0:chan].astype(BF16)
        for m in range(1, COUNT):
            part = d_inv[DEGREE[m] * chan : (DEGREE[m] + 1) * chan]
            grad_s[c, m] = (2.0 * msg[m] * part).astype(BF16)
        return active

    def backward(c, g):
        first = c * cand + g * CHUNK
        d_radial = [[[], [], []] for _ in range(CHUNK)]
        touched = [[None] * COUNT for _ in range(CHUNK)]
        for k in range(CHUNK):
            for m in range(COUNT):
                weight = jnp.broadcast_to(ysc[m, pl.ds(first + k, 1), :], (16, cap))
                wts[first + k, 16 * m : 16 * m + 16, :] = weight.astype(BF16)
        for s in range(chan // 16):
            at = slice(16 * s, 16 * s + 16)
            grads = [grad_s[c, m, at, :] for m in range(COUNT)]
            for k in range(CHUNK):
                sums = [None, None, None]
                value = [prod[first + k, d * chan + 16 * s : d * chan + 16 * s + 16, :] for d in range(3)]
                for m in range(COUNT):
                    d = DEGREE[m]
                    term = grads[m] * wts[first + k, 16 * m : 16 * m + 16, :]
                    sums[d] = term if sums[d] is None else sums[d] + term
                    change = value[d] * grads[m]
                    touched[k][m] = change if touched[k][m] is None else touched[k][m] + change
                feat = feat_s[first + k, at, :]
                for d in range(3):
                    d_radial[k][d].append(sums[d] * feat)
        d_radial = [jnp.concatenate([p for q in parts for p in q], axis=0) for parts in d_radial]
        touched = [jnp.concatenate(parts, axis=0) for parts in touched]
        d_hidden = dot(w_out[...], jnp.concatenate(d_radial, axis=1)).astype(BF16)
        d_pre = d_hidden * jnp.concatenate([slope[first + k] for k in range(CHUNK)], axis=1)
        d_basis = dot(w_in_half, d_pre).astype(BF16).astype(F32)
        sums = dot(adders, jnp.concatenate(touched, axis=1))
        for k in range(CHUNK):
            gsc[pl.ds((first + k) * 16, 16), :] = sums[:, k * cap : (k + 1) * cap]
            piece = d_basis[:, k * cap : (k + 1) * cap] * edge_s[first + k]
            rows_s[1, pl.ds(first + k, 1), :] = jnp.sum(piece, axis=0, keepdims=True)

    sub = lax.broadcasted_iota(jnp.int32, (8, cap), 0) & 3
    forces = {c: [None] * 3 for c in near}

    def finish(c, g):
        at = pl.ds(c * cand + g * 8, 8)
        x, y, w, squared, rest, envelope = [v[g * 8 : g * 8 + 8] for v in geometry[c]]
        grads = [gsc[pl.ds((c * cand + g * 8) * 16 + m, 8, stride=16), :] for m in range(COUNT)]
        d_env = grads[0]
        for m, value in enumerate(harmonics(x, y, w)):
            if m:
                d_env = d_env + value * grads[m]
        d_sq = 2.0 * (-2.0 * sharp * rows_s[1, at, :] - 3.0 * rest * rest * d_env)
        h = [None] + [envelope * grads[m] for m in range(1, 9)]
        gx = x * d_sq + h[1] + SQRT3 * (y * h[4] + w * h[6] + x * h[7]) - x * h[8]
        gy = y * d_sq + h[2] + SQRT3 * (x * h[4] + w * h[5] - y * h[7]) - y * h[8]
        gz = w * d_sq + h[3] + SQRT3 * (y * h[5] + x * h[6]) + 2.0 * w * h[8]
        for d, value in enumerate((gx, gy, gz)):
            rows_s[2 + d, at, :] = value
            forces[c][d] = value if forces[c][d] is None else forces[c][d] + value
        spread = []
        for r in range(c * cand + g * 8, c * cand + g * 8 + 8):
            row = [jnp.broadcast_to(rows_s[2 + d, pl.ds(r, 1), :], (8, cap)) for d in range(3)]
            block = jnp.where(sub == 0, row[0], jnp.where(sub == 1, row[1], row[2]))
            block = jnp.concatenate([block, block], axis=0).astype(BF16)
            spread.append(jnp.concatenate([chosen[r, 16 * t : 16 * t + 16, :] * block for t in range(tiles)], axis=0))
        slots = jnp.concatenate([onehot[r] for r in range(c * cand + g * 8, c * cand + g * 8 + 8)], axis=0)
        return dot(jnp.concatenate(spread, axis=1), slots)

    groups = cand // CHUNK
    active = {}
    for c in near:
        for g in range(groups):
            forward(c, g)
    for c in near:
        active[c] = node(c)
    scattered = None
    for c in near:
        for g in range(groups):
            backward(c, g)
            if (g + 1) * CHUNK % 8 == 0:
                part = finish(c, (g + 1) * CHUNK // 8 - 1)
                scattered = part if scattered is None else scattered + part
    for i in range(len(plan)):
        back[i] = scattered[4 * i : 4 * i + 4]
    returns = []
    for n, (step, there, own, length) in enumerate(runs):
        copy = pltpu.make_async_remote_copy(
            src_ref=back.at[pl.ds(there, length)],
            dst_ref=landed.at[pl.ds(there, length)],
            send_sem=send_b.at[n],
            recv_sem=recv_b.at[n],
            device_id=device(step),
            device_id_type=MESH,
        )
        copy.start()
        returns.append(copy)
    for c, (a, b, z) in enumerate(inner_cells):
        site_energy[a, b, pl.ds(z, 1), :] = rows[c][2] * jnp.sum(energy_col * active[c], axis=0, keepdims=True)
        forces[c] = [jnp.sum(g, axis=0, keepdims=True) for g in forces[c]]
    for copy in copies:
        copy.wait_send()
    for copy in returns:
        copy.wait_recv()
    for c, (a, b, z) in enumerate(inner_cells):
        kind, mass, occ, moved, half = rows[c]
        total = jnp.zeros((4, cap), F32)
        for i, (_, _, inner) in enumerate(plan):
            if inner == (a, b, z):
                total = total + (landed[i] if i in arriving else back[i])
        for d in range(3):
            force = occ * (forces[c][d] - total[d : d + 1])
            next_force[d, a, b, pl.ds(z, 1), :] = force
            next_velocity[d, a, b, pl.ds(z, 1), :] = occ * (half[d] + 0.5 * TIME_STEP * force / mass)
    for copy in returns:
        copy.wait_send()


def hand_over(*refs):
    half = len(refs) // 2
    for source, target in zip(refs[:half], refs[half:]):
        target[...] = source[...]


def solution(mesh):
    sizes = tuple(mesh.shape[a] for a in AXES)

    def shards(frac, velocity, force_old, species, cell_count, neighbours, embed, w_in, w_out, w_node, w_energy):
        cells, cap = species.shape[:3], species.shape[3]
        cand, chan, nb = neighbours.shape[0], embed.shape[1], w_in.shape[0]
        _, _, plan = halo_plan(cells, sizes)
        count = cells[0] * cells[1] * cells[2]
        pair_rows = count * cand
        held = len(plan)
        vmem = pl.BlockSpec(memory_space=pltpu.VMEM)
        operands = (frac, velocity, force_old, species, cell_count, neighbours)
        operands += (embed, w_in, w_out, w_node.T, w_energy.reshape(1, -1))
        operands = tuple(pltpu.with_memory_space_constraint(o, pltpu.HBM) for o in operands)
        staged = [pltpu.VMEM(o.shape, o.dtype) for o in operands]
        staged[4] = pltpu.SMEM(cell_count.shape, cell_count.dtype)
        field = jax.ShapeDtypeStruct(frac.shape, F32)
        results = (field, field, field, jax.ShapeDtypeStruct(species.shape, F32))
        outs = pl.pallas_call(
            functools.partial(step_kernel, sizes),
            out_shape=results,
            in_specs=[pl.BlockSpec(memory_space=pl.ANY)] * INPUTS,
            out_specs=(vmem,) * 4,
            scratch_shapes=staged
            + [
                pltpu.VMEM((held, 4, cap), F32),
                pltpu.VMEM((held, 4, cap), F32),
                pltpu.VMEM((held, 4, cap), F32),
                pltpu.VMEM((pair_rows, nb, cap), F32),
                pltpu.VMEM((COUNT, pair_rows, cap), F32),
                pltpu.VMEM((16 * pair_rows, cap), F32),
                pltpu.VMEM((5, pair_rows, cap), F32),
                pltpu.VMEM((3, pair_rows, cap), jnp.int32),
                pltpu.VMEM((count, COUNT, chan, cap), F32),
                pltpu.VMEM((chan, cap), F32),
                pltpu.SemaphoreType.DMA((held,)),
                pltpu.SemaphoreType.DMA((held,)),
                pltpu.SemaphoreType.DMA((held,)),
                pltpu.SemaphoreType.DMA((held,)),
                pltpu.SemaphoreType.DMA((INPUTS,)),
            ],
            compiler_params=pltpu.CompilerParams(
                collective_id=0, has_side_effects=True, vmem_limit_bytes=32 * 1024 * 1024
            ),
        )(*operands)
        return pl.pallas_call(
            hand_over,
            out_shape=results,
            in_specs=[vmem] * 4,
            out_specs=(vmem,) * 4,
            compiler_params=pltpu.CompilerParams(vmem_limit_bytes=1024 * 1024),
        )(*outs)

    field = P(None, "gx", "gy", "gz", None)
    cell = P("gx", "gy", "gz", None)
    return jax.shard_map(
        shards,
        mesh=mesh,
        in_specs=(field, field, field, cell, P("gx", "gy", "gz"), field, P(), P(), P(), P(), P()),
        out_specs=(field, field, field, cell),
        check_vma=False,
    )
```

```python
import functools
import itertools

import jax
import jax.numpy as jnp
from jax import lax
from jax.experimental import pallas as pl
from jax.experimental.pallas import tpu as pltpu
from jax.sharding import PartitionSpec as P

MASSES = (1.008, 12.011, 14.007, 15.999, 32.06, 22.99, 35.45, 39.098, 24.305, 40.078)
SQRT3 = 1.7320508075688772
HALF_SQRT3 = 0.8660254037844386
TIME_STEP = 0.5
AXES = ("gx", "gy", "gz")
MESH = pl.DeviceIdType.MESH
F32 = jnp.float32
BF16 = jnp.bfloat16
QUAD = 4
INPUTS = 11


def canonical(coordinate, cells, total):
    return coordinate % total if total < cells + 2 else coordinate


def halo_plan(cells, sizes):
    totals = [c * s for c, s in zip(cells, sizes)]
    spans = [sorted({canonical(e, c, t) for e in range(-1, c + 1)}) for c, t in zip(cells, totals)]
    plan = []
    for at in itertools.product(*spans):
        step = tuple(e // c for e, c in zip(at, cells))
        inner = tuple(e % c for e, c in zip(at, cells))
        plan.append((at, step, inner))
    return spans, totals, plan


def dot(a, b, ca=1, cb=0):
    return lax.dot_general(a, b, (((ca,), (cb,)), ((), ())), preferred_element_type=F32)


def silu_parts(pre):
    sig = 0.5 * jnp.tanh(0.5 * pre) + 0.5
    return pre * sig, sig * (1.0 + pre * (1.0 - sig))


def harmonics(x, y, z):
    return (
        None,
        x,
        y,
        z,
        SQRT3 * x * y,
        SQRT3 * y * z,
        SQRT3 * z * x,
        HALF_SQRT3 * (x * x - y * y),
        0.5 * (2.0 * z * z - x * x - y * y),
    )


DEGREE = (0, 1, 1, 1, 2, 2, 2, 2, 2)
COUNT = len(DEGREE)


def message_groups(plan, index_of, sizes):
    moves = [(i, step, index_of[inner]) for i, (_, step, inner) in enumerate(plan)]
    runs = []
    for i, step, own in moves:
        if not any(s % n for s, n in zip(step, sizes)):
            continue
        last = runs[-1] if runs else None
        if last and last[0] == step and last[1] + last[3] == i and last[2] + last[3] == own:
            runs[-1] = (step, last[1], last[2], last[3] + 1)
        else:
            runs.append((step, i, own, 1))
    return runs


def step_kernel(sizes, *refs):
    count = refs[3].shape[0] * refs[3].shape[1] * refs[3].shape[2]
    cap, cand, chan = refs[3].shape[3], refs[5].shape[0], refs[6].shape[1]
    spread_rows = refs[INPUTS + 4 + INPUTS + 1].shape[0] * 4
    spread_rows = -(-spread_rows // 16) * 16
    pair_rows = count * cand
    pl.run_scoped(
        functools.partial(step_body, sizes, refs),
        pltpu.VMEM((pair_rows, cap, cap), BF16),
        pltpu.VMEM((pair_rows, spread_rows, cap), BF16),
        pltpu.VMEM((pair_rows, 3 * chan, cap), BF16),
        pltpu.VMEM((pair_rows, chan, cap), BF16),
        pltpu.VMEM((pair_rows, chan, cap), BF16),
        pltpu.VMEM((pair_rows, 16 * COUNT, cap), BF16),
        pltpu.VMEM((count, COUNT, chan, cap), BF16),
    )


def step_body(sizes, refs, onehot, chosen, prod, feat_s, slope, wts, grad_s):
    sources, outs, held = refs[:INPUTS], refs[INPUTS : INPUTS + 4], refs[INPUTS + 4 :]
    next_frac, next_velocity, next_force, site_energy = outs
    staged, held = held[:INPUTS], held[INPUTS:]
    frac, velocity, force_old, species, cell_count, neighbours, embed, w_in, w_out, w_node_t, w_energy = staged
    table, back, landed, edge_s, ysc, gsc, rows_s, ints_s, msg_s, embed_t, columns_s, w_node_s = held[:12]
    send_a, recv_a, send_b, recv_b, load_sem = held[12:]
    cells = species.shape[:3]
    cap = species.shape[3]
    cand = neighbours.shape[0]
    chan = embed.shape[1]
    kinds = embed.shape[0]
    nb = w_in.shape[0]
    spans, totals, plan = halo_plan(cells, sizes)
    index_of = {at: i for i, (at, _, _) in enumerate(plan)}
    inner_cells = list(itertools.product(*[range(c) for c in cells]))
    me = [lax.axis_index(a) for a in AXES]

    def device(step):
        return {
            a: lax.rem(m + s + n, n) for a, m, s, n in zip(AXES, me, step, sizes)
        }

    runs = message_groups(plan, index_of, sizes)
    runs = sorted(runs, key=lambda r: (r[0][2] == 0, r[0][0] == 0))
    others = sorted({tuple(s % n for s, n in zip(step, sizes)) for step, _, _, _ in runs})
    barrier = pltpu.get_barrier_semaphore()
    for step in others:
        pl.semaphore_signal(barrier, inc=1, device_id=device(step), device_id_type=MESH)
    loads = [pltpu.make_async_copy(sources[i], staged[i], load_sem.at[i]) for i in range(INPUTS)]
    for load in loads:
        load.start()
    for load in loads[:5]:
        load.wait()

    rows = {}
    for c, (a, b, z) in enumerate(inner_cells):
        kind = species[a, b, pl.ds(z, 1), :]
        mass = jnp.zeros((1, cap), F32)
        for n, value in enumerate(MASSES):
            mass = jnp.where(kind == n, value / 16.0, mass)
        lane = lax.broadcasted_iota(jnp.int32, (1, cap), 1)
        occ = (lane < cell_count[a, b, z]).astype(F32)
        e = index_of[(a, b, z)]
        moved, half = [], []
        for d in range(3):
            h = velocity[d, a, b, pl.ds(z, 1), :] + 0.5 * TIME_STEP * force_old[d, a, b, pl.ds(z, 1), :] / mass
            m = frac[d, a, b, pl.ds(z, 1), :] + TIME_STEP * h
            table[e, d : d + 1, :] = m
            next_frac[d, a, b, pl.ds(z, 1), :] = occ * m
            half.append(h)
            moved.append(m)
        table[e, 3:4, :] = kind.astype(F32)
        rows[c] = (kind, mass, occ, moved, half)

    pl.semaphore_wait(barrier, len(others))
    copies = []
    for n, (step, there, own, length) in enumerate(runs):
        copy = pltpu.make_async_remote_copy(
            src_ref=table.at[pl.ds(own, length)],
            dst_ref=table.at[pl.ds(there, length)],
            send_sem=send_a.at[n],
            recv_sem=recv_a.at[n],
            device_id=device(tuple(-s for s in step)),
            device_id_type=MESH,
        )
        copy.start()
        copies.append(copy)

    for load in loads[5:]:
        load.wait()
    shift_bits = cap.bit_length() - 1
    pairs = {}
    slot_lanes = lax.broadcasted_iota(jnp.int32, (cap, cap), 1)
    tiles = chosen.shape[1] // 16
    quarter = lax.broadcasted_iota(jnp.int32, (16, cap), 0) >> 2
    for c, (a, b, z) in enumerate(inner_cells):
        at = pl.ds(c * cand, cand)
        for k in range(cand):
            ints_s[0, pl.ds(c * cand + k, 1), :] = neighbours[k, a, b, pl.ds(z, 1), :]
        code = ints_s[0, at, :]
        if cap == 1 << shift_bits:
            offset, slot = code >> shift_bits, code & (cap - 1)
        else:
            offset, slot = code // cap, code % cap
        third = (offset * 43) >> 7
        ninth = (offset * 57) >> 9
        shifts = (ninth - 1, third - 3 * ninth - 1, offset - 3 * third - 1)
        cell = jnp.zeros_like(code)
        for axis in range(3):
            place = (a, b, z)[axis] + shifts[axis]
            low = spans[axis][0]
            if totals[axis] < cells[axis] + 2:
                place = jnp.where(place < 0, place + totals[axis], place)
                place = jnp.where(place >= totals[axis], place - totals[axis], place)
            cell = cell * len(spans[axis]) + (place - low)
        ints_s[2, at, :] = cell
        pairs[c] = (slot, cell, [s.astype(F32) for s in shifts])
        columns_s[c] = jnp.concatenate([slot, jnp.zeros((cap - cand, cap), jnp.int32)], axis=0).T
        for k in range(cand):
            hit = jnp.broadcast_to(columns_s[c, :, k : k + 1], (cap, cap)) == slot_lanes
            onehot[c * cand + k] = jnp.where(hit, 1.0, 0.0).astype(BF16)

    def choose(r, carry):
        where = jnp.broadcast_to(ints_s[2, pl.ds(r, 1), :], (16, cap)) - quarter
        for t in range(tiles):
            chosen[r, 16 * t : 16 * t + 16, :] = jnp.where(where == 4 * t, 1.0, 0.0).astype(BF16)
        return carry

    lax.fori_loop(0, len(inner_cells) * cand, choose, 0)
    w_node_s[...] = w_node_t[:, 0 : 3 * chan].astype(F32).T.astype(BF16)

    w_in_half = (0.5 * w_in[...].astype(F32)).astype(BF16)
    w_in_t = (0.5 * w_in[...].astype(F32)).T.astype(BF16)
    w_out_t = w_out[...].astype(F32).T.astype(BF16)
    diag = lax.broadcasted_iota(jnp.int32, (chan, chan), 0) == lax.broadcasted_iota(jnp.int32, (chan, chan), 1)
    energy_row = jnp.broadcast_to(w_energy[...], (chan, chan))
    energy_col = jnp.sum(jnp.where(diag, energy_row, 0.0), axis=1, keepdims=True)
    kind_rows = lax.broadcasted_iota(jnp.int32, (kinds, cap), 0)
    centres = lax.broadcasted_iota(jnp.int32, (nb, cap), 0).astype(F32) / (nb - 1)
    kind_lanes = lax.broadcasted_iota(jnp.int32, (kinds, cap), 1)
    embed_t[...] = dot(embed[...], (kind_rows == kind_lanes).astype(F32).astype(BF16), 0, 0)
    own_feat = {
        c: dot(embed[...], (kind_rows == rows[c][0]).astype(F32).astype(BF16), 0, 0).astype(BF16)
        for c in rows
    }
    adders = jnp.where(
        lax.broadcasted_iota(jnp.int32, (16, COUNT * 16), 1) // 16
        == lax.broadcasted_iota(jnp.int32, (16, COUNT * 16), 0),
        1.0,
        0.0,
    ).astype(BF16)

    near = {
        c: {
            index_of[tuple(canonical(p + s, n, t) for p, s, n, t in zip(at, move, cells, totals))]
            for move in itertools.product((-1, 0, 1), repeat=3)
        }
        for c, at in enumerate(inner_cells)
    }
    found = {c: [jnp.zeros((cand, cap), F32) for _ in range(4)] for c in near}

    def take(cells_here):
        for e in cells_here:
            for c in near:
                if e in near[c]:
                    slot, cell, _ = pairs[c]
                    hit = cell == e
                    for q in range(4):
                        row = jnp.broadcast_to(table[e, q : q + 1, :], (cand, cap))
                        found[c][q] = jnp.where(hit, jnp.take_along_axis(row, slot, axis=1), found[c][q])

    arriving = {there + j for _, there, _, length in runs for j in range(length)}
    take([i for i in range(len(plan)) if i not in arriving])
    for flat in (True, False):
        group = [n for n, r in enumerate(runs) if (r[0][2] == 0) == flat]
        for n in group:
            copies[n].wait_recv()
        take([runs[n][1] + j for n in group for j in range(runs[n][3])])

    geometry = {}
    for c in near:
        slot, cell, shifts = pairs[c]
        x, y, w = [s + f - m for s, f, m in zip(shifts, found[c], rows[c][3])]
        squared = x * x + y * y + w * w
        rest = jnp.maximum(1.0 - squared, 0.0)
        envelope = rest * rest * rest
        geometry[c] = (x, y, w, squared, rest, envelope)
        at = pl.ds(c * cand, cand)
        rows_s[0, at, :] = squared
        ints_s[0, at, :] = found[c][3].astype(jnp.int32)
        for m, value in enumerate(harmonics(x, y, w)):
            ysc[m, at, :] = envelope if value is None else value * envelope

    sharp = float((nb - 1) ** 2)

    def forward(first, length):
        basis = []
        for k in range(length):
            gap = rows_s[0, pl.ds(first + k, 1), :] - centres
            value = jnp.exp(-sharp * (gap * gap))
            edge_s[first + k] = value * gap
            basis.append(value.astype(BF16))
        half = dot(w_in_t, jnp.concatenate(basis, axis=1))
        t = jnp.tanh(half)
        up = 1.0 + t
        hidden = half * up
        tilt = (up + hidden * (1.0 - t)).astype(BF16)
        for k in range(length):
            slope[first + k] = tilt[:, k * cap : (k + 1) * cap]
        radial = dot(w_out_t, hidden.astype(BF16)).astype(BF16)
        weight = []
        for k in range(length):
            row = []
            for m in range(COUNT):
                value = jnp.broadcast_to(ysc[m, pl.ds(first + k, 1), :], (16, cap)).astype(BF16)
                wts[first + k, 16 * m : 16 * m + 16, :] = value
                row.append(value)
            weight.append(row)
        for s in range(chan // 16):
            top = 16 * s
            carried = [[], [], []]
            for k in range(length):
                kind = jnp.broadcast_to(ints_s[0, pl.ds(first + k, 1), :], (16, cap))
                feat = jnp.take_along_axis(embed_t[top : top + 16, :], kind, axis=1).astype(BF16)
                feat_s[first + k, top : top + 16, :] = feat
                for d in range(3):
                    value = radial[d * chan + top : d * chan + top + 16, k * cap : (k + 1) * cap] * feat
                    prod[first + k, d * chan + top : d * chan + top + 16, :] = value
                    carried[d].append(value)
            for base in range(0, length, cand):
                for m in range(COUNT):
                    total = None
                    for low in range(base, base + cand, QUAD):
                        terms = [carried[DEGREE[m]][k] * weight[k][m] for k in range(low, low + QUAD)]
                        while len(terms) > 1:
                            terms = [p + q for p, q in zip(terms[::2], terms[1::2])]
                        part = terms[0].astype(F32)
                        total = part if total is None else total + part
                    msg_s[(first + base) // cand, m, top : top + 16, :] = total

    def node(c):
        occ = rows[c][2]
        msg = [msg_s[c, m] for m in range(COUNT)]
        vector = msg[1] * msg[1] + msg[2] * msg[2] + msg[3] * msg[3]
        tensor = msg[4] * msg[4]
        for m in range(5, 9):
            tensor = tensor + msg[m] * msg[m]
        invariant = jnp.concatenate([msg[0].astype(BF16), vector.astype(BF16), tensor.astype(BF16), own_feat[c]], axis=0)
        active, tilt = silu_parts(dot(w_node_t[...], invariant))
        d_pre = (energy_col * occ * tilt).astype(BF16)
        d_inv = dot(w_node_s[...], d_pre).astype(BF16).astype(F32)
        grad_s[c, 0] = d_inv[0:chan].astype(BF16)
        for m in range(1, COUNT):
            part = d_inv[DEGREE[m] * chan : (DEGREE[m] + 1) * chan]
            grad_s[c, m] = (2.0 * msg[m] * part).astype(BF16)
        return active

    def backward(first, length):
        d_radial = [[[], [], []] for _ in range(length)]
        touched = [[None] * COUNT for _ in range(length)]
        for k in range(length):
            for m in range(COUNT):
                weight = jnp.broadcast_to(ysc[m, pl.ds(first + k, 1), :], (16, cap))
                wts[first + k, 16 * m : 16 * m + 16, :] = weight.astype(BF16)
        for s in range(chan // 16):
            at = slice(16 * s, 16 * s + 16)
            for k in range(length):
                if k % cand == 0:
                    grads = [grad_s[(first + k) // cand, m, at, :] for m in range(COUNT)]
                sums = [None, None, None]
                value = [prod[first + k, d * chan + 16 * s : d * chan + 16 * s + 16, :] for d in range(3)]
                for m in range(COUNT):
                    d = DEGREE[m]
                    term = grads[m] * wts[first + k, 16 * m : 16 * m + 16, :]
                    sums[d] = term if sums[d] is None else sums[d] + term
                    change = value[d] * grads[m]
                    touched[k][m] = change if touched[k][m] is None else touched[k][m] + change
                feat = feat_s[first + k, at, :]
                for d in range(3):
                    d_radial[k][d].append(sums[d] * feat)
        d_radial = [jnp.concatenate([p for q in parts for p in q], axis=0) for parts in d_radial]
        touched = [jnp.concatenate(parts, axis=0) for parts in touched]
        d_hidden = dot(w_out[...], jnp.concatenate(d_radial, axis=1)).astype(BF16)
        d_pre = d_hidden * jnp.concatenate([slope[first + k] for k in range(length)], axis=1)
        d_basis = dot(w_in_half, d_pre).astype(BF16).astype(F32)
        sums = dot(adders, jnp.concatenate(touched, axis=1))
        for k in range(length):
            gsc[pl.ds((first + k) * 16, 16), :] = sums[:, k * cap : (k + 1) * cap]
            piece = d_basis[:, k * cap : (k + 1) * cap] * edge_s[first + k]
            rows_s[1, pl.ds(first + k, 1), :] = jnp.sum(piece, axis=0, keepdims=True)

    sub = lax.broadcasted_iota(jnp.int32, (8, cap), 0) & 3
    forces = {c: [None] * 3 for c in near}

    def finish(c, g):
        at = pl.ds(c * cand + g * 8, 8)
        x, y, w, squared, rest, envelope = [v[g * 8 : g * 8 + 8] for v in geometry[c]]
        grads = [gsc[pl.ds((c * cand + g * 8) * 16 + m, 8, stride=16), :] for m in range(COUNT)]
        d_env = grads[0]
        for m, value in enumerate(harmonics(x, y, w)):
            if m:
                d_env = d_env + value * grads[m]
        d_sq = 2.0 * (-2.0 * sharp * rows_s[1, at, :] - 3.0 * rest * rest * d_env)
        h = [None] + [envelope * grads[m] for m in range(1, 9)]
        gx = x * d_sq + h[1] + SQRT3 * (y * h[4] + w * h[6] + x * h[7]) - x * h[8]
        gy = y * d_sq + h[2] + SQRT3 * (x * h[4] + w * h[5] - y * h[7]) - y * h[8]
        gz = w * d_sq + h[3] + SQRT3 * (y * h[5] + x * h[6]) + 2.0 * w * h[8]
        for d, value in enumerate((gx, gy, gz)):
            rows_s[2 + d, at, :] = value
            forces[c][d] = value if forces[c][d] is None else forces[c][d] + value
        spread = []
        for r in range(c * cand + g * 8, c * cand + g * 8 + 8):
            row = [jnp.broadcast_to(rows_s[2 + d, pl.ds(r, 1), :], (8, cap)) for d in range(3)]
            block = jnp.where(sub == 0, row[0], jnp.where(sub == 1, row[1], row[2]))
            block = jnp.concatenate([block, block], axis=0).astype(BF16)
            spread.append(jnp.concatenate([chosen[r, 16 * t : 16 * t + 16, :] * block for t in range(tiles)], axis=0))
        slots = jnp.concatenate([onehot[r] for r in range(c * cand + g * 8, c * cand + g * 8 + 8)], axis=0)
        return jnp.concatenate(spread, axis=1), slots

    active = {}
    for c in near:
        forward(c * cand, cand)
    for c in near:
        active[c] = node(c)
    for c in near:
        backward(c * cand, cand)
    pieces = [finish(c, g) for c in near for g in range(cand // 8)]
    scattered = dot(jnp.concatenate([p[0] for p in pieces], axis=1), jnp.concatenate([p[1] for p in pieces], axis=0))
    for i in range(len(plan)):
        back[i] = scattered[4 * i : 4 * i + 4]
    returns = []
    for n, (step, there, own, length) in enumerate(runs):
        copy = pltpu.make_async_remote_copy(
            src_ref=back.at[pl.ds(there, length)],
            dst_ref=landed.at[pl.ds(there, length)],
            send_sem=send_b.at[n],
            recv_sem=recv_b.at[n],
            device_id=device(step),
            device_id_type=MESH,
        )
        copy.start()
        returns.append(copy)
    for c, (a, b, z) in enumerate(inner_cells):
        site_energy[a, b, pl.ds(z, 1), :] = rows[c][2] * jnp.sum(energy_col * active[c], axis=0, keepdims=True)
        forces[c] = [jnp.sum(g, axis=0, keepdims=True) for g in forces[c]]
    for copy in copies:
        copy.wait_send()
    for copy in returns:
        copy.wait_recv()
    for c, (a, b, z) in enumerate(inner_cells):
        kind, mass, occ, moved, half = rows[c]
        total = jnp.zeros((4, cap), F32)
        for i, (_, _, inner) in enumerate(plan):
            if inner == (a, b, z):
                total = total + (landed[i] if i in arriving else back[i])
        for d in range(3):
            force = occ * (forces[c][d] - total[d : d + 1])
            next_force[d, a, b, pl.ds(z, 1), :] = force
            next_velocity[d, a, b, pl.ds(z, 1), :] = occ * (half[d] + 0.5 * TIME_STEP * force / mass)
    for copy in returns:
        copy.wait_send()


def hand_over(*refs):
    half = len(refs) // 2
    for source, target in zip(refs[:half], refs[half:]):
        target[...] = source[...]


def solution(mesh):
    sizes = tuple(mesh.shape[a] for a in AXES)

    def shards(frac, velocity, force_old, species, cell_count, neighbours, embed, w_in, w_out, w_node, w_energy):
        cells, cap = species.shape[:3], species.shape[3]
        cand, chan, nb = neighbours.shape[0], embed.shape[1], w_in.shape[0]
        _, _, plan = halo_plan(cells, sizes)
        count = cells[0] * cells[1] * cells[2]
        pair_rows = count * cand
        held = len(plan)
        vmem = pl.BlockSpec(memory_space=pltpu.VMEM)
        operands = (frac, velocity, force_old, species, cell_count, neighbours)
        operands += (embed, w_in, w_out, w_node.T, w_energy.reshape(1, -1))
        operands = tuple(pltpu.with_memory_space_constraint(o, pltpu.HBM) for o in operands)
        staged = [pltpu.VMEM(o.shape, o.dtype) for o in operands]
        staged[4] = pltpu.SMEM(cell_count.shape, cell_count.dtype)
        field = jax.ShapeDtypeStruct(frac.shape, F32)
        results = (field, field, field, jax.ShapeDtypeStruct(species.shape, F32))
        outs = pl.pallas_call(
            functools.partial(step_kernel, sizes),
            out_shape=results,
            in_specs=[pl.BlockSpec(memory_space=pl.ANY)] * INPUTS,
            out_specs=(vmem,) * 4,
            scratch_shapes=staged
            + [
                pltpu.VMEM((held, 4, cap), F32),
                pltpu.VMEM((held, 4, cap), F32),
                pltpu.VMEM((held, 4, cap), F32),
                pltpu.VMEM((pair_rows, nb, cap), F32),
                pltpu.VMEM((COUNT, pair_rows, cap), F32),
                pltpu.VMEM((16 * pair_rows, cap), F32),
                pltpu.VMEM((5, pair_rows, cap), F32),
                pltpu.VMEM((3, pair_rows, cap), jnp.int32),
                pltpu.VMEM((count, COUNT, chan, cap), F32),
                pltpu.VMEM((chan, cap), F32),
                pltpu.VMEM((count, cap, cap), jnp.int32),
                pltpu.VMEM((3 * chan, chan), BF16),
                pltpu.SemaphoreType.DMA((held,)),
                pltpu.SemaphoreType.DMA((held,)),
                pltpu.SemaphoreType.DMA((held,)),
                pltpu.SemaphoreType.DMA((held,)),
                pltpu.SemaphoreType.DMA((INPUTS,)),
            ],
            compiler_params=pltpu.CompilerParams(
                collective_id=0, has_side_effects=True, vmem_limit_bytes=32 * 1024 * 1024
            ),
        )(*operands)
        return pl.pallas_call(
            hand_over,
            out_shape=results,
            in_specs=[vmem] * 4,
            out_specs=(vmem,) * 4,
            compiler_params=pltpu.CompilerParams(vmem_limit_bytes=1024 * 1024),
        )(*outs)

    field = P(None, "gx", "gy", "gz", None)
    cell = P("gx", "gy", "gz", None)
    return jax.shard_map(
        shards,
        mesh=mesh,
        in_specs=(field, field, field, cell, P("gx", "gy", "gz"), field, P(), P(), P(), P(), P()),
        out_specs=(field, field, field, cell),
        check_vma=False,
    )
```

```python
import functools
import itertools

import jax
import jax.numpy as jnp
from jax import lax
from jax.experimental import pallas as pl
from jax.experimental.pallas import tpu as pltpu
from jax.sharding import PartitionSpec as P

MASSES = (1.008, 12.011, 14.007, 15.999, 32.06, 22.99, 35.45, 39.098, 24.305, 40.078)
SQRT3 = 1.7320508075688772
HALF_SQRT3 = 0.8660254037844386
TIME_STEP = 0.5
AXES = ("gx", "gy", "gz")
MESH = pl.DeviceIdType.MESH
F32 = jnp.float32
BF16 = jnp.bfloat16
QUAD = 16
INPUTS = 11


def canonical(coordinate, cells, total):
    return coordinate % total if total < cells + 2 else coordinate


def halo_plan(cells, sizes):
    totals = [c * s for c, s in zip(cells, sizes)]
    spans = [sorted({canonical(e, c, t) for e in range(-1, c + 1)}) for c, t in zip(cells, totals)]
    plan = []
    for at in itertools.product(*spans):
        step = tuple(e // c for e, c in zip(at, cells))
        inner = tuple(e % c for e, c in zip(at, cells))
        plan.append((at, step, inner))
    return spans, totals, plan


def dot(a, b, ca=1, cb=0):
    return lax.dot_general(a, b, (((ca,), (cb,)), ((), ())), preferred_element_type=F32)


def silu_parts(pre):
    sig = 0.5 * jnp.tanh(0.5 * pre) + 0.5
    return pre * sig, sig * (1.0 + pre * (1.0 - sig))


def harmonics(x, y, z):
    return (
        None,
        x,
        y,
        z,
        SQRT3 * x * y,
        SQRT3 * y * z,
        SQRT3 * z * x,
        HALF_SQRT3 * (x * x - y * y),
        0.5 * (2.0 * z * z - x * x - y * y),
    )


DEGREE = (0, 1, 1, 1, 2, 2, 2, 2, 2)
COUNT = len(DEGREE)


def message_groups(plan, index_of, sizes):
    moves = [(i, step, index_of[inner]) for i, (_, step, inner) in enumerate(plan)]
    runs = []
    for i, step, own in moves:
        if not any(s % n for s, n in zip(step, sizes)):
            continue
        last = runs[-1] if runs else None
        if last and last[0] == step and last[1] + last[3] == i and last[2] + last[3] == own:
            runs[-1] = (step, last[1], last[2], last[3] + 1)
        else:
            runs.append((step, i, own, 1))
    return runs


def step_kernel(sizes, *refs):
    count = refs[3].shape[0] * refs[3].shape[1] * refs[3].shape[2]
    cap, cand, chan = refs[3].shape[3], refs[5].shape[0], refs[6].shape[1]
    spread_rows = refs[INPUTS + 4 + INPUTS + 1].shape[0] * 4
    spread_rows = -(-spread_rows // 16) * 16
    pair_rows = count * cand
    pl.run_scoped(
        functools.partial(step_body, sizes, refs),
        pltpu.VMEM((pair_rows, cap, cap), BF16),
        pltpu.VMEM((pair_rows, spread_rows, cap), BF16),
        pltpu.VMEM((pair_rows, 3 * chan, cap), BF16),
        pltpu.VMEM((pair_rows, chan, cap), BF16),
        pltpu.VMEM((pair_rows, chan, cap), BF16),
        pltpu.VMEM((pair_rows, 16 * COUNT, cap), BF16),
        pltpu.VMEM((count, COUNT, chan, cap), BF16),
    )


def step_body(sizes, refs, onehot, chosen, prod, feat_s, slope, wts, grad_s):
    sources, outs, held = refs[:INPUTS], refs[INPUTS : INPUTS + 4], refs[INPUTS + 4 :]
    next_frac, next_velocity, next_force, site_energy = outs
    staged, held = held[:INPUTS], held[INPUTS:]
    frac, velocity, force_old, species, cell_count, neighbours, embed, w_in, w_out, w_node_t, w_energy = staged
    table, back, landed, edge_s, ysc, gsc, rows_s, ints_s, msg_s, embed_t, columns_s, w_node_s = held[:12]
    send_a, recv_a, send_b, recv_b, load_sem = held[12:]
    cells = species.shape[:3]
    cap = species.shape[3]
    cand = neighbours.shape[0]
    chan = embed.shape[1]
    kinds = embed.shape[0]
    nb = w_in.shape[0]
    spans, totals, plan = halo_plan(cells, sizes)
    index_of = {at: i for i, (at, _, _) in enumerate(plan)}
    inner_cells = list(itertools.product(*[range(c) for c in cells]))
    me = [lax.axis_index(a) for a in AXES]

    def device(step):
        return {
            a: lax.rem(m + s + n, n) for a, m, s, n in zip(AXES, me, step, sizes)
        }

    runs = message_groups(plan, index_of, sizes)
    runs = sorted(runs, key=lambda r: (r[0][2] == 0, r[0][0] == 0))
    others = sorted({tuple(s % n for s, n in zip(step, sizes)) for step, _, _, _ in runs})
    others = sorted(others, key=lambda s: (s[2] == 0, s[0] == 0))
    barrier = pltpu.get_barrier_semaphore()
    for step in others:
        pl.semaphore_signal(barrier, inc=1, device_id=device(step), device_id_type=MESH)
    loads = [pltpu.make_async_copy(sources[i], staged[i], load_sem.at[i]) for i in range(INPUTS)]
    for load in loads:
        load.start()
    for load in loads[:5]:
        load.wait()

    rows = {}
    for c, (a, b, z) in enumerate(inner_cells):
        kind = species[a, b, pl.ds(z, 1), :]
        mass = jnp.zeros((1, cap), F32)
        for n, value in enumerate(MASSES):
            mass = jnp.where(kind == n, value / 16.0, mass)
        lane = lax.broadcasted_iota(jnp.int32, (1, cap), 1)
        occ = (lane < cell_count[a, b, z]).astype(F32)
        e = index_of[(a, b, z)]
        moved, half = [], []
        for d in range(3):
            h = velocity[d, a, b, pl.ds(z, 1), :] + 0.5 * TIME_STEP * force_old[d, a, b, pl.ds(z, 1), :] / mass
            m = frac[d, a, b, pl.ds(z, 1), :] + TIME_STEP * h
            table[e, d : d + 1, :] = m
            next_frac[d, a, b, pl.ds(z, 1), :] = occ * m
            half.append(h)
            moved.append(m)
        table[e, 3:4, :] = kind.astype(F32)
        rows[c] = (kind, mass, occ, moved, half)

    pl.semaphore_wait(barrier, len(others))
    copies = []
    for n, (step, there, own, length) in enumerate(runs):
        copy = pltpu.make_async_remote_copy(
            src_ref=table.at[pl.ds(own, length)],
            dst_ref=table.at[pl.ds(there, length)],
            send_sem=send_a.at[n],
            recv_sem=recv_a.at[n],
            device_id=device(tuple(-s for s in step)),
            device_id_type=MESH,
        )
        copy.start()
        copies.append(copy)

    for load in loads[5:]:
        load.wait()
    shift_bits = cap.bit_length() - 1
    pairs = {}
    slot_lanes = lax.broadcasted_iota(jnp.int32, (cap, cap), 1)
    tiles = chosen.shape[1] // 16
    quarter = lax.broadcasted_iota(jnp.int32, (16, cap), 0) >> 2
    for c, (a, b, z) in enumerate(inner_cells):
        at = pl.ds(c * cand, cand)
        for k in range(cand):
            ints_s[0, pl.ds(c * cand + k, 1), :] = neighbours[k, a, b, pl.ds(z, 1), :]
        code = ints_s[0, at, :]
        if cap == 1 << shift_bits:
            offset, slot = code >> shift_bits, code & (cap - 1)
        else:
            offset, slot = code // cap, code % cap
        third = (offset * 43) >> 7
        ninth = (offset * 57) >> 9
        shifts = (ninth - 1, third - 3 * ninth - 1, offset - 3 * third - 1)
        cell = jnp.zeros_like(code)
        for axis in range(3):
            place = (a, b, z)[axis] + shifts[axis]
            low = spans[axis][0]
            if totals[axis] < cells[axis] + 2:
                place = jnp.where(place < 0, place + totals[axis], place)
                place = jnp.where(place >= totals[axis], place - totals[axis], place)
            cell = cell * len(spans[axis]) + (place - low)
        ints_s[2, at, :] = cell
        pairs[c] = (slot, cell, [s.astype(F32) for s in shifts])
        columns_s[c] = jnp.concatenate([slot, jnp.zeros((cap - cand, cap), jnp.int32)], axis=0).T
        for k in range(cand):
            hit = jnp.broadcast_to(columns_s[c, :, k : k + 1], (cap, cap)) == slot_lanes
            onehot[c * cand + k] = jnp.where(hit, 1.0, 0.0).astype(BF16)

    def choose(r, carry):
        where = jnp.broadcast_to(ints_s[2, pl.ds(r, 1), :], (16, cap)) - quarter
        for t in range(tiles):
            chosen[r, 16 * t : 16 * t + 16, :] = jnp.where(where == 4 * t, 1.0, 0.0).astype(BF16)
        return carry

    lax.fori_loop(0, len(inner_cells) * cand, choose, 0)
    w_node_s[...] = w_node_t[:, 0 : 3 * chan].astype(F32).T.astype(BF16)

    w_in_half = (0.5 * w_in[...].astype(F32)).astype(BF16)
    w_in_t = (0.5 * w_in[...].astype(F32)).T.astype(BF16)
    w_out_t = w_out[...].astype(F32).T.astype(BF16)
    diag = lax.broadcasted_iota(jnp.int32, (chan, chan), 0) == lax.broadcasted_iota(jnp.int32, (chan, chan), 1)
    energy_row = jnp.broadcast_to(w_energy[...], (chan, chan))
    energy_col = jnp.sum(jnp.where(diag, energy_row, 0.0), axis=1, keepdims=True)
    kind_rows = lax.broadcasted_iota(jnp.int32, (kinds, cap), 0)
    centres = lax.broadcasted_iota(jnp.int32, (nb, cap), 0).astype(F32) / (nb - 1)
    kind_lanes = lax.broadcasted_iota(jnp.int32, (kinds, cap), 1)
    embed_t[...] = dot(embed[...], (kind_rows == kind_lanes).astype(F32).astype(BF16), 0, 0)
    own_feat = {
        c: dot(embed[...], (kind_rows == rows[c][0]).astype(F32).astype(BF16), 0, 0).astype(BF16)
        for c in rows
    }
    adders = jnp.where(
        lax.broadcasted_iota(jnp.int32, (16, COUNT * 16), 1) // 16
        == lax.broadcasted_iota(jnp.int32, (16, COUNT * 16), 0),
        1.0,
        0.0,
    ).astype(BF16)

    near = {
        c: {
            index_of[tuple(canonical(p + s, n, t) for p, s, n, t in zip(at, move, cells, totals))]
            for move in itertools.product((-1, 0, 1), repeat=3)
        }
        for c, at in enumerate(inner_cells)
    }
    found = {c: [jnp.zeros((cand, cap), F32) for _ in range(4)] for c in near}

    def take(cells_here):
        for e in cells_here:
            for c in near:
                if e in near[c]:
                    slot, cell, _ = pairs[c]
                    hit = cell == e
                    for q in range(4):
                        row = jnp.broadcast_to(table[e, q : q + 1, :], (cand, cap))
                        found[c][q] = jnp.where(hit, jnp.take_along_axis(row, slot, axis=1), found[c][q])

    arriving = {there + j for _, there, _, length in runs for j in range(length)}
    take([i for i in range(len(plan)) if i not in arriving])
    stages = [(z, x) for z in (True, False) for x in (True, False)]
    for stage in stages:
        group = [n for n, r in enumerate(runs) if (r[0][2] == 0, r[0][0] == 0) == stage]
        for n in group:
            copies[n].wait_recv()
        take([runs[n][1] + j for n in group for j in range(runs[n][3])])

    geometry = {}
    for c in near:
        slot, cell, shifts = pairs[c]
        x, y, w = [s + f - m for s, f, m in zip(shifts, found[c], rows[c][3])]
        squared = x * x + y * y + w * w
        rest = jnp.maximum(1.0 - squared, 0.0)
        envelope = rest * rest * rest
        geometry[c] = (x, y, w, squared, rest, envelope)
        at = pl.ds(c * cand, cand)
        rows_s[0, at, :] = squared
        ints_s[0, at, :] = found[c][3].astype(jnp.int32)
        for m, value in enumerate(harmonics(x, y, w)):
            ysc[m, at, :] = envelope if value is None else value * envelope

    sharp = float((nb - 1) ** 2)

    def forward(first, length):
        basis = []
        for k in range(length):
            gap = rows_s[0, pl.ds(first + k, 1), :] - centres
            value = jnp.exp(-sharp * (gap * gap))
            edge_s[first + k] = value * gap
            basis.append(value.astype(BF16))
        half = dot(w_in_t, jnp.concatenate(basis, axis=1))
        t = jnp.tanh(half)
        up = 1.0 + t
        hidden = half * up
        tilt = (up + hidden * (1.0 - t)).astype(BF16)
        for k in range(length):
            slope[first + k] = tilt[:, k * cap : (k + 1) * cap]
        radial = dot(w_out_t, hidden.astype(BF16)).astype(BF16)
        weight = []
        for k in range(length):
            row = []
            for m in range(COUNT):
                value = jnp.broadcast_to(ysc[m, pl.ds(first + k, 1), :], (16, cap)).astype(BF16)
                wts[first + k, 16 * m : 16 * m + 16, :] = value
                row.append(value)
            weight.append(row)
        for s in range(chan // 16):
            top = 16 * s
            carried = [[], [], []]
            for k in range(length):
                kind = jnp.broadcast_to(ints_s[0, pl.ds(first + k, 1), :], (16, cap))
                feat = jnp.take_along_axis(embed_t[top : top + 16, :], kind, axis=1).astype(BF16)
                feat_s[first + k, top : top + 16, :] = feat
                for d in range(3):
                    value = radial[d * chan + top : d * chan + top + 16, k * cap : (k + 1) * cap] * feat
                    prod[first + k, d * chan + top : d * chan + top + 16, :] = value
                    carried[d].append(value)
            for base in range(0, length, cand):
                for m in range(COUNT):
                    total = None
                    for low in range(base, base + cand, QUAD):
                        terms = [carried[DEGREE[m]][k] * weight[k][m] for k in range(low, low + QUAD)]
                        while len(terms) > 1:
                            terms = [p + q for p, q in zip(terms[::2], terms[1::2])]
                        part = terms[0].astype(F32)
                        total = part if total is None else total + part
                    msg_s[(first + base) // cand, m, top : top + 16, :] = total

    def node(c):
        occ = rows[c][2]
        msg = [msg_s[c, m] for m in range(COUNT)]
        vector = msg[1] * msg[1] + msg[2] * msg[2] + msg[3] * msg[3]
        tensor = msg[4] * msg[4]
        for m in range(5, 9):
            tensor = tensor + msg[m] * msg[m]
        invariant = jnp.concatenate([msg[0].astype(BF16), vector.astype(BF16), tensor.astype(BF16), own_feat[c]], axis=0)
        active, tilt = silu_parts(dot(w_node_t[...], invariant))
        d_pre = (energy_col * occ * tilt).astype(BF16)
        d_inv = dot(w_node_s[...], d_pre).astype(BF16).astype(F32)
        grad_s[c, 0] = d_inv[0:chan].astype(BF16)
        for m in range(1, COUNT):
            part = d_inv[DEGREE[m] * chan : (DEGREE[m] + 1) * chan]
            grad_s[c, m] = (2.0 * msg[m] * part).astype(BF16)
        return active

    def backward(first, length):
        d_radial = [[[], [], []] for _ in range(length)]
        touched = [[None] * COUNT for _ in range(length)]
        for k in range(length):
            for m in range(COUNT):
                weight = jnp.broadcast_to(ysc[m, pl.ds(first + k, 1), :], (16, cap))
                wts[first + k, 16 * m : 16 * m + 16, :] = weight.astype(BF16)
        for s in range(chan // 16):
            at = slice(16 * s, 16 * s + 16)
            for k in range(length):
                if k % cand == 0:
                    grads = [grad_s[(first + k) // cand, m, at, :] for m in range(COUNT)]
                sums = [None, None, None]
                value = [prod[first + k, d * chan + 16 * s : d * chan + 16 * s + 16, :] for d in range(3)]
                for m in range(COUNT):
                    d = DEGREE[m]
                    term = grads[m] * wts[first + k, 16 * m : 16 * m + 16, :]
                    sums[d] = term if sums[d] is None else sums[d] + term
                    change = value[d] * grads[m]
                    touched[k][m] = change if touched[k][m] is None else touched[k][m] + change
                feat = feat_s[first + k, at, :]
                for d in range(3):
                    d_radial[k][d].append(sums[d] * feat)
        d_radial = [jnp.concatenate([p for q in parts for p in q], axis=0) for parts in d_radial]
        touched = [jnp.concatenate(parts, axis=0) for parts in touched]
        d_hidden = dot(w_out[...], jnp.concatenate(d_radial, axis=1)).astype(BF16)
        d_pre = d_hidden * jnp.concatenate([slope[first + k] for k in range(length)], axis=1)
        d_basis = dot(w_in_half, d_pre).astype(BF16).astype(F32)
        sums = dot(adders, jnp.concatenate(touched, axis=1))
        for k in range(length):
            gsc[pl.ds((first + k) * 16, 16), :] = sums[:, k * cap : (k + 1) * cap]
            piece = d_basis[:, k * cap : (k + 1) * cap] * edge_s[first + k]
            rows_s[1, pl.ds(first + k, 1), :] = jnp.sum(piece, axis=0, keepdims=True)

    sub = lax.broadcasted_iota(jnp.int32, (8, cap), 0) & 3
    forces = {c: [None] * 3 for c in near}

    def finish(c, g):
        at = pl.ds(c * cand + g * 8, 8)
        x, y, w, squared, rest, envelope = [v[g * 8 : g * 8 + 8] for v in geometry[c]]
        grads = [gsc[pl.ds((c * cand + g * 8) * 16 + m, 8, stride=16), :] for m in range(COUNT)]
        d_env = grads[0]
        for m, value in enumerate(harmonics(x, y, w)):
            if m:
                d_env = d_env + value * grads[m]
        d_sq = 2.0 * (-2.0 * sharp * rows_s[1, at, :] - 3.0 * rest * rest * d_env)
        h = [None] + [envelope * grads[m] for m in range(1, 9)]
        gx = x * d_sq + h[1] + SQRT3 * (y * h[4] + w * h[6] + x * h[7]) - x * h[8]
        gy = y * d_sq + h[2] + SQRT3 * (x * h[4] + w * h[5] - y * h[7]) - y * h[8]
        gz = w * d_sq + h[3] + SQRT3 * (y * h[5] + x * h[6]) + 2.0 * w * h[8]
        for d, value in enumerate((gx, gy, gz)):
            rows_s[2 + d, at, :] = value
            forces[c][d] = value if forces[c][d] is None else forces[c][d] + value
        spread = []
        for r in range(c * cand + g * 8, c * cand + g * 8 + 8):
            row = [jnp.broadcast_to(rows_s[2 + d, pl.ds(r, 1), :], (8, cap)) for d in range(3)]
            block = jnp.where(sub == 0, row[0], jnp.where(sub == 1, row[1], row[2]))
            block = jnp.concatenate([block, block], axis=0).astype(BF16)
            spread.append(jnp.concatenate([chosen[r, 16 * t : 16 * t + 16, :] * block for t in range(tiles)], axis=0))
        slots = jnp.concatenate([onehot[r] for r in range(c * cand + g * 8, c * cand + g * 8 + 8)], axis=0)
        return jnp.concatenate(spread, axis=1), slots

    active = {}
    for c in near:
        forward(c * cand, cand)
    for c in near:
        active[c] = node(c)
    for c in near:
        backward(c * cand, cand)
    pieces = [finish(c, g) for c in near for g in range(cand // 8)]
    scattered = dot(jnp.concatenate([p[0] for p in pieces], axis=1), jnp.concatenate([p[1] for p in pieces], axis=0))
    for i in range(len(plan)):
        back[i] = scattered[4 * i : 4 * i + 4]
    returns = []
    for n, (step, there, own, length) in enumerate(runs):
        copy = pltpu.make_async_remote_copy(
            src_ref=back.at[pl.ds(there, length)],
            dst_ref=landed.at[pl.ds(there, length)],
            send_sem=send_b.at[n],
            recv_sem=recv_b.at[n],
            device_id=device(step),
            device_id_type=MESH,
        )
        copy.start()
        returns.append(copy)
    for c, (a, b, z) in enumerate(inner_cells):
        site_energy[a, b, pl.ds(z, 1), :] = rows[c][2] * jnp.sum(energy_col * active[c], axis=0, keepdims=True)
        forces[c] = [jnp.sum(g, axis=0, keepdims=True) for g in forces[c]]
    totals_here = {}
    for c, at in enumerate(inner_cells):
        gain = rows[c][2] * (0.5 * TIME_STEP) / rows[c][1]
        own = [i for i, (_, _, inner) in enumerate(plan) if inner == at and i not in arriving]
        totals_here[c] = (sum(back[i] for i in own), gain, [rows[c][2] * h for h in rows[c][4]])
    for copy in copies:
        copy.wait_send()
    for copy in returns:
        copy.wait_send()
    for stage in stages:
        group = [n for n, r in enumerate(runs) if (r[0][2] == 0, r[0][0] == 0) == stage]
        for n in group:
            returns[n].wait_recv()
        for c, at in enumerate(inner_cells):
            total, gain, half = totals_here[c]
            for n in group:
                for j in range(runs[n][3]):
                    if plan[runs[n][1] + j][2] == at:
                        total = total + landed[runs[n][1] + j]
            totals_here[c] = (total, gain, half)
    for c, (a, b, z) in enumerate(inner_cells):
        total, gain, half = totals_here[c]
        for d in range(3):
            force = forces[c][d] - total[d : d + 1]
            next_force[d, a, b, pl.ds(z, 1), :] = rows[c][2] * force
            next_velocity[d, a, b, pl.ds(z, 1), :] = half[d] + gain * force


def hand_over(*refs):
    half = len(refs) // 2
    for source, target in zip(refs[:half], refs[half:]):
        target[...] = source[...]


def solution(mesh):
    sizes = tuple(mesh.shape[a] for a in AXES)

    def shards(frac, velocity, force_old, species, cell_count, neighbours, embed, w_in, w_out, w_node, w_energy):
        cells, cap = species.shape[:3], species.shape[3]
        cand, chan, nb = neighbours.shape[0], embed.shape[1], w_in.shape[0]
        _, _, plan = halo_plan(cells, sizes)
        count = cells[0] * cells[1] * cells[2]
        pair_rows = count * cand
        held = len(plan)
        vmem = pl.BlockSpec(memory_space=pltpu.VMEM)
        operands = (frac, velocity, force_old, species, cell_count, neighbours)
        operands += (embed, w_in, w_out, w_node.T, w_energy.reshape(1, -1))
        operands = tuple(pltpu.with_memory_space_constraint(o, pltpu.HBM) for o in operands)
        staged = [pltpu.VMEM(o.shape, o.dtype) for o in operands]
        staged[4] = pltpu.SMEM(cell_count.shape, cell_count.dtype)
        field = jax.ShapeDtypeStruct(frac.shape, F32)
        results = (field, field, field, jax.ShapeDtypeStruct(species.shape, F32))
        outs = pl.pallas_call(
            functools.partial(step_kernel, sizes),
            out_shape=results,
            in_specs=[pl.BlockSpec(memory_space=pl.ANY)] * INPUTS,
            out_specs=(vmem,) * 4,
            scratch_shapes=staged
            + [
                pltpu.VMEM((held, 4, cap), F32),
                pltpu.VMEM((held, 4, cap), F32),
                pltpu.VMEM((held, 4, cap), F32),
                pltpu.VMEM((pair_rows, nb, cap), F32),
                pltpu.VMEM((COUNT, pair_rows, cap), F32),
                pltpu.VMEM((16 * pair_rows, cap), F32),
                pltpu.VMEM((5, pair_rows, cap), F32),
                pltpu.VMEM((3, pair_rows, cap), jnp.int32),
                pltpu.VMEM((count, COUNT, chan, cap), F32),
                pltpu.VMEM((chan, cap), F32),
                pltpu.VMEM((count, cap, cap), jnp.int32),
                pltpu.VMEM((3 * chan, chan), BF16),
                pltpu.SemaphoreType.DMA((held,)),
                pltpu.SemaphoreType.DMA((held,)),
                pltpu.SemaphoreType.DMA((held,)),
                pltpu.SemaphoreType.DMA((held,)),
                pltpu.SemaphoreType.DMA((INPUTS,)),
            ],
            compiler_params=pltpu.CompilerParams(
                collective_id=0, has_side_effects=True, vmem_limit_bytes=32 * 1024 * 1024
            ),
        )(*operands)
        return pl.pallas_call(
            hand_over,
            out_shape=results,
            in_specs=[vmem] * 4,
            out_specs=(vmem,) * 4,
            compiler_params=pltpu.CompilerParams(vmem_limit_bytes=1024 * 1024),
        )(*outs)

    field = P(None, "gx", "gy", "gz", None)
    cell = P("gx", "gy", "gz", None)
    return jax.shard_map(
        shards,
        mesh=mesh,
        in_specs=(field, field, field, cell, P("gx", "gy", "gz"), field, P(), P(), P(), P(), P()),
        out_specs=(field, field, field, cell),
        check_vma=False,
    )
```

```python
import functools
import itertools

import jax
import jax.numpy as jnp
from jax import lax
from jax.experimental import pallas as pl
from jax.experimental.pallas import tpu as pltpu
from jax.sharding import PartitionSpec as P

MASSES = (1.008, 12.011, 14.007, 15.999, 32.06, 22.99, 35.45, 39.098, 24.305, 40.078)
SQRT3 = 1.7320508075688772
HALF_SQRT3 = 0.8660254037844386
TIME_STEP = 0.5
AXES = ("gx", "gy", "gz")
MESH = pl.DeviceIdType.MESH
F32 = jnp.float32
BF16 = jnp.bfloat16
QUAD = 16
INPUTS = 11


def canonical(coordinate, cells, total):
    return coordinate % total if total < cells + 2 else coordinate


def halo_plan(cells, sizes):
    totals = [c * s for c, s in zip(cells, sizes)]
    spans = [sorted({canonical(e, c, t) for e in range(-1, c + 1)}) for c, t in zip(cells, totals)]
    plan = []
    for at in itertools.product(*spans):
        step = tuple(e // c for e, c in zip(at, cells))
        inner = tuple(e % c for e, c in zip(at, cells))
        plan.append((at, step, inner))
    return spans, totals, plan


def dot(a, b, ca=1, cb=0):
    return lax.dot_general(a, b, (((ca,), (cb,)), ((), ())), preferred_element_type=F32)


def silu_parts(pre):
    sig = 0.5 * jnp.tanh(0.5 * pre) + 0.5
    return pre * sig, sig * (1.0 + pre * (1.0 - sig))


def harmonics(x, y, z):
    return (
        None,
        x,
        y,
        z,
        SQRT3 * x * y,
        SQRT3 * y * z,
        SQRT3 * z * x,
        HALF_SQRT3 * (x * x - y * y),
        0.5 * (2.0 * z * z - x * x - y * y),
    )


DEGREE = (0, 1, 1, 1, 2, 2, 2, 2, 2)
COUNT = len(DEGREE)


def message_groups(plan, index_of, sizes):
    moves = [(i, step, index_of[inner]) for i, (_, step, inner) in enumerate(plan)]
    runs = []
    for i, step, own in moves:
        if not any(s % n for s, n in zip(step, sizes)):
            continue
        last = runs[-1] if runs else None
        if last and last[0] == step and last[1] + last[3] == i and last[2] + last[3] == own:
            runs[-1] = (step, last[1], last[2], last[3] + 1)
        else:
            runs.append((step, i, own, 1))
    return runs


def step_kernel(sizes, *refs):
    count = refs[3].shape[0] * refs[3].shape[1] * refs[3].shape[2]
    cap, cand, chan = refs[3].shape[3], refs[5].shape[0], refs[6].shape[1]
    spread_rows = refs[INPUTS + 4 + INPUTS + 1].shape[0] * 4
    spread_rows = -(-spread_rows // 16) * 16
    pair_rows = count * cand
    pl.run_scoped(
        functools.partial(step_body, sizes, refs),
        pltpu.VMEM((pair_rows, cap, cap), BF16),
        pltpu.VMEM((pair_rows, spread_rows, cap), BF16),
        pltpu.VMEM((pair_rows, 3 * chan, cap), BF16),
        pltpu.VMEM((pair_rows, chan, cap), BF16),
        pltpu.VMEM((pair_rows, chan, cap), BF16),
        pltpu.VMEM((pair_rows, 16 * COUNT, cap), BF16),
        pltpu.VMEM((count, COUNT, chan, cap), BF16),
    )


def step_body(sizes, refs, onehot, chosen, prod, feat_s, slope, wts, grad_s):
    sources, outs, held = refs[:INPUTS], refs[INPUTS : INPUTS + 4], refs[INPUTS + 4 :]
    next_frac, next_velocity, next_force, site_energy = outs
    staged, held = held[:INPUTS], held[INPUTS:]
    frac, velocity, force_old, species, cell_count, neighbours, embed, w_in, w_out, w_node_t, w_energy = staged
    table, back, landed, edge_s, ysc, gsc, rows_s, ints_s, msg_s, embed_t, columns_s, w_node_s = held[:12]
    send_a, recv_a, send_b, recv_b, load_sem = held[12:]
    cells = species.shape[:3]
    cap = species.shape[3]
    cand = neighbours.shape[0]
    chan = embed.shape[1]
    kinds = embed.shape[0]
    nb = w_in.shape[0]
    spans, totals, plan = halo_plan(cells, sizes)
    index_of = {at: i for i, (at, _, _) in enumerate(plan)}
    inner_cells = list(itertools.product(*[range(c) for c in cells]))
    me = [lax.axis_index(a) for a in AXES]

    def device(step):
        return {
            a: lax.rem(m + s + n, n) for a, m, s, n in zip(AXES, me, step, sizes)
        }

    runs = message_groups(plan, index_of, sizes)
    runs = sorted(runs, key=lambda r: (r[0][2] == 0, r[0][0] == 0))
    others = sorted({tuple(s % n for s, n in zip(step, sizes)) for step, _, _, _ in runs})
    others = sorted(others, key=lambda s: (s[2] == 0, s[0] == 0))
    barrier = pltpu.get_barrier_semaphore()
    for step in others:
        pl.semaphore_signal(barrier, inc=1, device_id=device(step), device_id_type=MESH)
    loads = [pltpu.make_async_copy(sources[i], staged[i], load_sem.at[i]) for i in range(INPUTS)]
    for load in loads:
        load.start()
    for load in loads[:5]:
        load.wait()

    rows = {}
    for c, (a, b, z) in enumerate(inner_cells):
        kind = species[a, b, pl.ds(z, 1), :]
        mass = jnp.zeros((1, cap), F32)
        for n, value in enumerate(MASSES):
            mass = jnp.where(kind == n, value / 16.0, mass)
        lane = lax.broadcasted_iota(jnp.int32, (1, cap), 1)
        occ = (lane < cell_count[a, b, z]).astype(F32)
        e = index_of[(a, b, z)]
        moved, half = [], []
        for d in range(3):
            h = velocity[d, a, b, pl.ds(z, 1), :] + 0.5 * TIME_STEP * force_old[d, a, b, pl.ds(z, 1), :] / mass
            m = frac[d, a, b, pl.ds(z, 1), :] + TIME_STEP * h
            table[e, d : d + 1, :] = m
            next_frac[d, a, b, pl.ds(z, 1), :] = occ * m
            half.append(h)
            moved.append(m)
        table[e, 3:4, :] = kind.astype(F32)
        rows[c] = (kind, mass, occ, moved, half)

    pl.semaphore_wait(barrier, len(others))
    copies = []
    for n, (step, there, own, length) in enumerate(runs):
        copy = pltpu.make_async_remote_copy(
            src_ref=table.at[pl.ds(own, length)],
            dst_ref=table.at[pl.ds(there, length)],
            send_sem=send_a.at[n],
            recv_sem=recv_a.at[n],
            device_id=device(tuple(-s for s in step)),
            device_id_type=MESH,
        )
        copy.start()
        copies.append(copy)

    for load in loads[5:]:
        load.wait()
    shift_bits = cap.bit_length() - 1
    pairs = {}
    slot_lanes = lax.broadcasted_iota(jnp.int32, (cap, cap), 1)
    tiles = chosen.shape[1] // 16
    quarter = lax.broadcasted_iota(jnp.int32, (16, cap), 0) >> 2
    for c, (a, b, z) in enumerate(inner_cells):
        at = pl.ds(c * cand, cand)
        for k in range(cand):
            ints_s[0, pl.ds(c * cand + k, 1), :] = neighbours[k, a, b, pl.ds(z, 1), :]
        code = ints_s[0, at, :]
        if cap == 1 << shift_bits:
            offset, slot = code >> shift_bits, code & (cap - 1)
        else:
            offset, slot = code // cap, code % cap
        third = (offset * 43) >> 7
        ninth = (offset * 57) >> 9
        shifts = (ninth - 1, third - 3 * ninth - 1, offset - 3 * third - 1)
        cell = jnp.zeros_like(code)
        for axis in range(3):
            place = (a, b, z)[axis] + shifts[axis]
            low = spans[axis][0]
            if totals[axis] < cells[axis] + 2:
                place = jnp.where(place < 0, place + totals[axis], place)
                place = jnp.where(place >= totals[axis], place - totals[axis], place)
            cell = cell * len(spans[axis]) + (place - low)
        ints_s[2, at, :] = cell
        pairs[c] = (slot, cell, [s.astype(F32) for s in shifts])
        columns_s[c] = jnp.concatenate([slot, jnp.zeros((cap - cand, cap), jnp.int32)], axis=0).T
        for k in range(cand):
            hit = jnp.broadcast_to(columns_s[c, :, k : k + 1], (cap, cap)) == slot_lanes
            onehot[c * cand + k] = jnp.where(hit, 1.0, 0.0).astype(BF16)

    def choose(r, carry):
        where = jnp.broadcast_to(ints_s[2, pl.ds(r, 1), :], (16, cap)) - quarter
        for t in range(tiles):
            chosen[r, 16 * t : 16 * t + 16, :] = jnp.where(where == 4 * t, 1.0, 0.0).astype(BF16)
        return carry

    lax.fori_loop(0, len(inner_cells) * cand, choose, 0)
    w_node_s[...] = w_node_t[:, 0 : 3 * chan].astype(F32).T.astype(BF16)

    w_in_half = (0.5 * w_in[...].astype(F32)).astype(BF16)
    w_in_t = (0.5 * w_in[...].astype(F32)).T.astype(BF16)
    w_out_t = w_out[...].astype(F32).T.astype(BF16)
    diag = lax.broadcasted_iota(jnp.int32, (chan, chan), 0) == lax.broadcasted_iota(jnp.int32, (chan, chan), 1)
    energy_row = jnp.broadcast_to(w_energy[...], (chan, chan))
    energy_col = jnp.sum(jnp.where(diag, energy_row, 0.0), axis=1, keepdims=True)
    kind_rows = lax.broadcasted_iota(jnp.int32, (kinds, cap), 0)
    centres = lax.broadcasted_iota(jnp.int32, (nb, cap), 0).astype(F32) / (nb - 1)
    kind_lanes = lax.broadcasted_iota(jnp.int32, (kinds, cap), 1)
    embed_t[...] = dot(embed[...], (kind_rows == kind_lanes).astype(F32).astype(BF16), 0, 0)
    own_feat = {
        c: dot(embed[...], (kind_rows == rows[c][0]).astype(F32).astype(BF16), 0, 0).astype(BF16)
        for c in rows
    }
    adders = jnp.where(
        lax.broadcasted_iota(jnp.int32, (16, COUNT * 16), 1) // 16
        == lax.broadcasted_iota(jnp.int32, (16, COUNT * 16), 0),
        1.0,
        0.0,
    ).astype(BF16)

    near = {
        c: {
            index_of[tuple(canonical(p + s, n, t) for p, s, n, t in zip(at, move, cells, totals))]
            for move in itertools.product((-1, 0, 1), repeat=3)
        }
        for c, at in enumerate(inner_cells)
    }
    found = {c: [jnp.zeros((cand, cap), F32) for _ in range(4)] for c in near}

    def take(cells_here):
        for e in cells_here:
            for c in near:
                if e in near[c]:
                    slot, cell, _ = pairs[c]
                    hit = cell == e
                    for q in range(4):
                        row = jnp.broadcast_to(table[e, q : q + 1, :], (cand, cap))
                        found[c][q] = jnp.where(hit, jnp.take_along_axis(row, slot, axis=1), found[c][q])

    arriving = {there + j for _, there, _, length in runs for j in range(length)}
    take([i for i in range(len(plan)) if i not in arriving])
    stages = [(z, x) for z in (True, False) for x in (True, False)]
    for stage in stages:
        group = [n for n, r in enumerate(runs) if (r[0][2] == 0, r[0][0] == 0) == stage]
        for n in group:
            copies[n].wait_recv()
        take([runs[n][1] + j for n in group for j in range(runs[n][3])])

    geometry = {}
    for c in near:
        slot, cell, shifts = pairs[c]
        x, y, w = [s + f - m for s, f, m in zip(shifts, found[c], rows[c][3])]
        squared = x * x + y * y + w * w
        rest = jnp.maximum(1.0 - squared, 0.0)
        envelope = rest * rest * rest
        geometry[c] = (x, y, w, squared, rest, envelope)
        at = pl.ds(c * cand, cand)
        rows_s[0, at, :] = squared
        ints_s[0, at, :] = found[c][3].astype(jnp.int32)
        for m, value in enumerate(harmonics(x, y, w)):
            ysc[m, at, :] = envelope if value is None else value * envelope

    sharp = float((nb - 1) ** 2)

    def forward(first, length):
        basis = []
        for k in range(length):
            gap = rows_s[0, pl.ds(first + k, 1), :] - centres
            value = jnp.exp(-sharp * (gap * gap))
            edge_s[first + k] = value * gap
            basis.append(value.astype(BF16))
        half = dot(w_in_t, jnp.concatenate(basis, axis=1))
        half = half.astype(BF16)
        t = jnp.tanh(half)
        up = 1.0 + t
        hidden = half * up
        tilt = up + hidden * (1.0 - t)
        for k in range(length):
            slope[first + k] = tilt[:, k * cap : (k + 1) * cap]
        radial = dot(w_out_t, hidden).astype(BF16)
        weight = []
        for k in range(length):
            row = []
            for m in range(COUNT):
                value = jnp.broadcast_to(ysc[m, pl.ds(first + k, 1), :], (16, cap)).astype(BF16)
                wts[first + k, 16 * m : 16 * m + 16, :] = value
                row.append(value)
            weight.append(row)
        for s in range(chan // 16):
            top = 16 * s
            carried = [[], [], []]
            for k in range(length):
                kind = jnp.broadcast_to(ints_s[0, pl.ds(first + k, 1), :], (16, cap))
                feat = jnp.take_along_axis(embed_t[top : top + 16, :], kind, axis=1).astype(BF16)
                feat_s[first + k, top : top + 16, :] = feat
                for d in range(3):
                    value = radial[d * chan + top : d * chan + top + 16, k * cap : (k + 1) * cap] * feat
                    prod[first + k, d * chan + top : d * chan + top + 16, :] = value
                    carried[d].append(value)
            for base in range(0, length, cand):
                for m in range(COUNT):
                    total = None
                    for low in range(base, base + cand, QUAD):
                        terms = [carried[DEGREE[m]][k] * weight[k][m] for k in range(low, low + QUAD)]
                        while len(terms) > 1:
                            terms = [p + q for p, q in zip(terms[::2], terms[1::2])]
                        part = terms[0].astype(F32)
                        total = part if total is None else total + part
                    msg_s[(first + base) // cand, m, top : top + 16, :] = total

    def node(c):
        occ = rows[c][2]
        msg = [msg_s[c, m] for m in range(COUNT)]
        vector = msg[1] * msg[1] + msg[2] * msg[2] + msg[3] * msg[3]
        tensor = msg[4] * msg[4]
        for m in range(5, 9):
            tensor = tensor + msg[m] * msg[m]
        invariant = jnp.concatenate([msg[0].astype(BF16), vector.astype(BF16), tensor.astype(BF16), own_feat[c]], axis=0)
        active, tilt = silu_parts(dot(w_node_t[...], invariant))
        d_pre = (energy_col * occ * tilt).astype(BF16)
        d_inv = dot(w_node_s[...], d_pre).astype(BF16).astype(F32)
        grad_s[c, 0] = d_inv[0:chan].astype(BF16)
        for m in range(1, COUNT):
            part = d_inv[DEGREE[m] * chan : (DEGREE[m] + 1) * chan]
            grad_s[c, m] = (2.0 * msg[m] * part).astype(BF16)
        return active

    def backward(first, length):
        d_radial = [[[], [], []] for _ in range(length)]
        touched = [[None] * COUNT for _ in range(length)]
        for k in range(length):
            for m in range(COUNT):
                weight = jnp.broadcast_to(ysc[m, pl.ds(first + k, 1), :], (16, cap))
                wts[first + k, 16 * m : 16 * m + 16, :] = weight.astype(BF16)
        for s in range(chan // 16):
            at = slice(16 * s, 16 * s + 16)
            for k in range(length):
                if k % cand == 0:
                    grads = [grad_s[(first + k) // cand, m, at, :] for m in range(COUNT)]
                sums = [None, None, None]
                value = [prod[first + k, d * chan + 16 * s : d * chan + 16 * s + 16, :] for d in range(3)]
                for m in range(COUNT):
                    d = DEGREE[m]
                    term = grads[m] * wts[first + k, 16 * m : 16 * m + 16, :]
                    sums[d] = term if sums[d] is None else sums[d] + term
                    change = value[d] * grads[m]
                    touched[k][m] = change if touched[k][m] is None else touched[k][m] + change
                feat = feat_s[first + k, at, :]
                for d in range(3):
                    d_radial[k][d].append(sums[d] * feat)
        d_radial = [jnp.concatenate([p for q in parts for p in q], axis=0) for parts in d_radial]
        touched = [jnp.concatenate(parts, axis=0) for parts in touched]
        d_hidden = dot(w_out[...], jnp.concatenate(d_radial, axis=1)).astype(BF16)
        d_pre = d_hidden * jnp.concatenate([slope[first + k] for k in range(length)], axis=1)
        d_basis = dot(w_in_half, d_pre).astype(BF16).astype(F32)
        sums = dot(adders, jnp.concatenate(touched, axis=1))
        for k in range(length):
            gsc[pl.ds((first + k) * 16, 16), :] = sums[:, k * cap : (k + 1) * cap]
            piece = d_basis[:, k * cap : (k + 1) * cap] * edge_s[first + k]
            rows_s[1, pl.ds(first + k, 1), :] = jnp.sum(piece, axis=0, keepdims=True)

    sub = lax.broadcasted_iota(jnp.int32, (8, cap), 0) & 3
    forces = {c: [None] * 3 for c in near}

    def finish(c, g):
        at = pl.ds(c * cand + g * 8, 8)
        x, y, w, squared, rest, envelope = [v[g * 8 : g * 8 + 8] for v in geometry[c]]
        grads = [gsc[pl.ds((c * cand + g * 8) * 16 + m, 8, stride=16), :] for m in range(COUNT)]
        d_env = grads[0]
        for m, value in enumerate(harmonics(x, y, w)):
            if m:
                d_env = d_env + value * grads[m]
        d_sq = 2.0 * (-2.0 * sharp * rows_s[1, at, :] - 3.0 * rest * rest * d_env)
        h = [None] + [envelope * grads[m] for m in range(1, 9)]
        gx = x * d_sq + h[1] + SQRT3 * (y * h[4] + w * h[6] + x * h[7]) - x * h[8]
        gy = y * d_sq + h[2] + SQRT3 * (x * h[4] + w * h[5] - y * h[7]) - y * h[8]
        gz = w * d_sq + h[3] + SQRT3 * (y * h[5] + x * h[6]) + 2.0 * w * h[8]
        for d, value in enumerate((gx, gy, gz)):
            rows_s[2 + d, at, :] = value
            forces[c][d] = value if forces[c][d] is None else forces[c][d] + value
        spread = []
        for r in range(c * cand + g * 8, c * cand + g * 8 + 8):
            row = [jnp.broadcast_to(rows_s[2 + d, pl.ds(r, 1), :], (8, cap)) for d in range(3)]
            block = jnp.where(sub == 0, row[0], jnp.where(sub == 1, row[1], row[2]))
            block = jnp.concatenate([block, block], axis=0).astype(BF16)
            spread.append(jnp.concatenate([chosen[r, 16 * t : 16 * t + 16, :] * block for t in range(tiles)], axis=0))
        slots = jnp.concatenate([onehot[r] for r in range(c * cand + g * 8, c * cand + g * 8 + 8)], axis=0)
        return jnp.concatenate(spread, axis=1), slots

    active = {}
    forward(0, len(near) * cand)
    for c in near:
        active[c] = node(c)
    for c in near:
        backward(c * cand, cand)
    pieces = [finish(c, g) for c in near for g in range(cand // 8)]
    scattered = dot(jnp.concatenate([p[0] for p in pieces], axis=1), jnp.concatenate([p[1] for p in pieces], axis=0))
    for i in range(len(plan)):
        back[i] = scattered[4 * i : 4 * i + 4]
    returns = []
    for n, (step, there, own, length) in enumerate(runs):
        copy = pltpu.make_async_remote_copy(
            src_ref=back.at[pl.ds(there, length)],
            dst_ref=landed.at[pl.ds(there, length)],
            send_sem=send_b.at[n],
            recv_sem=recv_b.at[n],
            device_id=device(step),
            device_id_type=MESH,
        )
        copy.start()
        returns.append(copy)
    for c, (a, b, z) in enumerate(inner_cells):
        site_energy[a, b, pl.ds(z, 1), :] = rows[c][2] * jnp.sum(energy_col * active[c], axis=0, keepdims=True)
        forces[c] = [jnp.sum(g, axis=0, keepdims=True) for g in forces[c]]
    totals_here = {}
    for c, at in enumerate(inner_cells):
        gain = rows[c][2] * (0.5 * TIME_STEP) / rows[c][1]
        own = [i for i, (_, _, inner) in enumerate(plan) if inner == at and i not in arriving]
        totals_here[c] = (sum(back[i] for i in own), gain, [rows[c][2] * h for h in rows[c][4]])
    for copy in copies:
        copy.wait_send()
    for copy in returns:
        copy.wait_send()
    for stage in stages:
        group = [n for n, r in enumerate(runs) if (r[0][2] == 0, r[0][0] == 0) == stage]
        for n in group:
            returns[n].wait_recv()
        for c, at in enumerate(inner_cells):
            total, gain, half = totals_here[c]
            for n in group:
                for j in range(runs[n][3]):
                    if plan[runs[n][1] + j][2] == at:
                        total = total + landed[runs[n][1] + j]
            totals_here[c] = (total, gain, half)
    for c, (a, b, z) in enumerate(inner_cells):
        total, gain, half = totals_here[c]
        for d in range(3):
            force = forces[c][d] - total[d : d + 1]
            next_force[d, a, b, pl.ds(z, 1), :] = rows[c][2] * force
            next_velocity[d, a, b, pl.ds(z, 1), :] = half[d] + gain * force


def hand_over(*refs):
    half = len(refs) // 2
    for source, target in zip(refs[:half], refs[half:]):
        target[...] = source[...]


def solution(mesh):
    sizes = tuple(mesh.shape[a] for a in AXES)

    def shards(frac, velocity, force_old, species, cell_count, neighbours, embed, w_in, w_out, w_node, w_energy):
        cells, cap = species.shape[:3], species.shape[3]
        cand, chan, nb = neighbours.shape[0], embed.shape[1], w_in.shape[0]
        _, _, plan = halo_plan(cells, sizes)
        count = cells[0] * cells[1] * cells[2]
        pair_rows = count * cand
        held = len(plan)
        vmem = pl.BlockSpec(memory_space=pltpu.VMEM)
        operands = (frac, velocity, force_old, species, cell_count, neighbours)
        operands += (embed, w_in, w_out, w_node.T, w_energy.reshape(1, -1))
        operands = tuple(pltpu.with_memory_space_constraint(o, pltpu.HBM) for o in operands)
        staged = [pltpu.VMEM(o.shape, o.dtype) for o in operands]
        staged[4] = pltpu.SMEM(cell_count.shape, cell_count.dtype)
        field = jax.ShapeDtypeStruct(frac.shape, F32)
        results = (field, field, field, jax.ShapeDtypeStruct(species.shape, F32))
        outs = pl.pallas_call(
            functools.partial(step_kernel, sizes),
            out_shape=results,
            in_specs=[pl.BlockSpec(memory_space=pl.ANY)] * INPUTS,
            out_specs=(vmem,) * 4,
            scratch_shapes=staged
            + [
                pltpu.VMEM((held, 4, cap), F32),
                pltpu.VMEM((held, 4, cap), F32),
                pltpu.VMEM((held, 4, cap), F32),
                pltpu.VMEM((pair_rows, nb, cap), F32),
                pltpu.VMEM((COUNT, pair_rows, cap), F32),
                pltpu.VMEM((16 * pair_rows, cap), F32),
                pltpu.VMEM((5, pair_rows, cap), F32),
                pltpu.VMEM((3, pair_rows, cap), jnp.int32),
                pltpu.VMEM((count, COUNT, chan, cap), F32),
                pltpu.VMEM((chan, cap), F32),
                pltpu.VMEM((count, cap, cap), jnp.int32),
                pltpu.VMEM((3 * chan, chan), BF16),
                pltpu.SemaphoreType.DMA((held,)),
                pltpu.SemaphoreType.DMA((held,)),
                pltpu.SemaphoreType.DMA((held,)),
                pltpu.SemaphoreType.DMA((held,)),
                pltpu.SemaphoreType.DMA((INPUTS,)),
            ],
            compiler_params=pltpu.CompilerParams(
                collective_id=0, has_side_effects=True, vmem_limit_bytes=32 * 1024 * 1024
            ),
        )(*operands)
        return pl.pallas_call(
            hand_over,
            out_shape=results,
            in_specs=[vmem] * 4,
            out_specs=(vmem,) * 4,
            compiler_params=pltpu.CompilerParams(vmem_limit_bytes=1024 * 1024),
        )(*outs)

    field = P(None, "gx", "gy", "gz", None)
    cell = P("gx", "gy", "gz", None)
    return jax.shard_map(
        shards,
        mesh=mesh,
        in_specs=(field, field, field, cell, P("gx", "gy", "gz"), field, P(), P(), P(), P(), P()),
        out_specs=(field, field, field, cell),
        check_vma=False,
    )
```

```python
import functools
import itertools

import jax
import jax.numpy as jnp
from jax import lax
from jax.experimental import pallas as pl
from jax.experimental.pallas import tpu as pltpu
from jax.sharding import PartitionSpec as P

MASSES = (1.008, 12.011, 14.007, 15.999, 32.06, 22.99, 35.45, 39.098, 24.305, 40.078)
SQRT3 = 1.7320508075688772
HALF_SQRT3 = 0.8660254037844386
TIME_STEP = 0.5
AXES = ("gx", "gy", "gz")
MESH = pl.DeviceIdType.MESH
F32 = jnp.float32
BF16 = jnp.bfloat16
QUAD = 16
INPUTS = 11


def canonical(coordinate, cells, total):
    return coordinate % total if total < cells + 2 else coordinate


def halo_plan(cells, sizes):
    totals = [c * s for c, s in zip(cells, sizes)]
    spans = [sorted({canonical(e, c, t) for e in range(-1, c + 1)}) for c, t in zip(cells, totals)]
    plan = []
    for at in itertools.product(*spans):
        step = tuple(e // c for e, c in zip(at, cells))
        inner = tuple(e % c for e, c in zip(at, cells))
        plan.append((at, step, inner))
    return spans, totals, plan


def dot(a, b, ca=1, cb=0):
    return lax.dot_general(a, b, (((ca,), (cb,)), ((), ())), preferred_element_type=F32)


def silu_parts(pre):
    sig = 0.5 * jnp.tanh(0.5 * pre) + 0.5
    return pre * sig, sig * (1.0 + pre * (1.0 - sig))


def harmonics(x, y, z):
    return (
        None,
        x,
        y,
        z,
        SQRT3 * x * y,
        SQRT3 * y * z,
        SQRT3 * z * x,
        HALF_SQRT3 * (x * x - y * y),
        0.5 * (2.0 * z * z - x * x - y * y),
    )


DEGREE = (0, 1, 1, 1, 2, 2, 2, 2, 2)
COUNT = len(DEGREE)


def message_groups(plan, index_of, sizes):
    moves = [(i, step, index_of[inner]) for i, (_, step, inner) in enumerate(plan)]
    runs = []
    for i, step, own in moves:
        if not any(s % n for s, n in zip(step, sizes)):
            continue
        last = runs[-1] if runs else None
        if last and last[0] == step and last[1] + last[3] == i and last[2] + last[3] == own:
            runs[-1] = (step, last[1], last[2], last[3] + 1)
        else:
            runs.append((step, i, own, 1))
    return runs


def step_kernel(sizes, *refs):
    count = refs[3].shape[0] * refs[3].shape[1] * refs[3].shape[2]
    cap, cand, chan = refs[3].shape[3], refs[5].shape[0], refs[6].shape[1]
    spread_rows = refs[INPUTS + 4 + INPUTS + 1].shape[0] * 4
    spread_rows = -(-spread_rows // 16) * 16
    pair_rows = count * cand
    pl.run_scoped(
        functools.partial(step_body, sizes, refs),
        pltpu.VMEM((pair_rows, cap, cap), BF16),
        pltpu.VMEM((pair_rows, spread_rows, cap), BF16),
        pltpu.VMEM((pair_rows, 3 * chan, cap), BF16),
        pltpu.VMEM((pair_rows, chan, cap), BF16),
        pltpu.VMEM((pair_rows, chan, cap), BF16),
        pltpu.VMEM((pair_rows, 16 * COUNT, cap), BF16),
        pltpu.VMEM((count, COUNT, chan, cap), BF16),
    )


def step_body(sizes, refs, onehot, chosen, prod, feat_s, slope, wts, grad_s):
    sources, outs, held = refs[:INPUTS], refs[INPUTS : INPUTS + 4], refs[INPUTS + 4 :]
    next_frac, next_velocity, next_force, site_energy = outs
    staged, held = held[:INPUTS], held[INPUTS:]
    frac, velocity, force_old, species, cell_count, neighbours, embed, w_in, w_out, w_node_t, w_energy = staged
    table, back, landed, edge_s, ysc, gsc, rows_s, ints_s, msg_s, embed_t, columns_s, w_node_s = held[:12]
    send_a, recv_a, send_b, recv_b, load_sem = held[12:]
    cells = species.shape[:3]
    cap = species.shape[3]
    cand = neighbours.shape[0]
    chan = embed.shape[1]
    kinds = embed.shape[0]
    nb = w_in.shape[0]
    spans, totals, plan = halo_plan(cells, sizes)
    index_of = {at: i for i, (at, _, _) in enumerate(plan)}
    inner_cells = list(itertools.product(*[range(c) for c in cells]))
    me = [lax.axis_index(a) for a in AXES]

    def device(step):
        return {
            a: lax.rem(m + s + n, n) for a, m, s, n in zip(AXES, me, step, sizes)
        }

    runs = message_groups(plan, index_of, sizes)
    runs = sorted(runs, key=lambda r: (r[0][2] == 0, r[0][0] == 0))
    others = sorted({tuple(s % n for s, n in zip(step, sizes)) for step, _, _, _ in runs})
    others = sorted(others, key=lambda s: (s[2] == 0, s[0] == 0))
    barrier = pltpu.get_barrier_semaphore()
    for step in others:
        pl.semaphore_signal(barrier, inc=1, device_id=device(step), device_id_type=MESH)
    loads = [pltpu.make_async_copy(sources[i], staged[i], load_sem.at[i]) for i in range(INPUTS)]
    for load in loads:
        load.start()
    for load in loads[:5]:
        load.wait()

    rows = {}
    for c, (a, b, z) in enumerate(inner_cells):
        kind = species[a, b, pl.ds(z, 1), :]
        mass = jnp.zeros((1, cap), F32)
        for n, value in enumerate(MASSES):
            mass = jnp.where(kind == n, value / 16.0, mass)
        lane = lax.broadcasted_iota(jnp.int32, (1, cap), 1)
        occ = (lane < cell_count[a, b, z]).astype(F32)
        e = index_of[(a, b, z)]
        moved, half = [], []
        for d in range(3):
            h = velocity[d, a, b, pl.ds(z, 1), :] + 0.5 * TIME_STEP * force_old[d, a, b, pl.ds(z, 1), :] / mass
            m = frac[d, a, b, pl.ds(z, 1), :] + TIME_STEP * h
            table[e, d : d + 1, :] = m
            next_frac[d, a, b, pl.ds(z, 1), :] = occ * m
            half.append(h)
            moved.append(m)
        table[e, 3:4, :] = kind.astype(F32)
        rows[c] = (kind, mass, occ, moved, half)

    pl.semaphore_wait(barrier, len(others))
    copies = []
    for n, (step, there, own, length) in enumerate(runs):
        copy = pltpu.make_async_remote_copy(
            src_ref=table.at[pl.ds(own, length)],
            dst_ref=table.at[pl.ds(there, length)],
            send_sem=send_a.at[n],
            recv_sem=recv_a.at[n],
            device_id=device(tuple(-s for s in step)),
            device_id_type=MESH,
        )
        copy.start()
        copies.append(copy)

    for load in loads[5:]:
        load.wait()
    shift_bits = cap.bit_length() - 1
    pairs = {}
    slot_lanes = lax.broadcasted_iota(jnp.int32, (cap, cap), 1)
    tiles = chosen.shape[1] // 16
    quarter = lax.broadcasted_iota(jnp.int32, (16, cap), 0) >> 2
    for c, (a, b, z) in enumerate(inner_cells):
        at = pl.ds(c * cand, cand)
        for k in range(cand):
            ints_s[0, pl.ds(c * cand + k, 1), :] = neighbours[k, a, b, pl.ds(z, 1), :]
        code = ints_s[0, at, :]
        if cap == 1 << shift_bits:
            offset, slot = code >> shift_bits, code & (cap - 1)
        else:
            offset, slot = code // cap, code % cap
        third = (offset * 43) >> 7
        ninth = (offset * 57) >> 9
        shifts = (ninth - 1, third - 3 * ninth - 1, offset - 3 * third - 1)
        cell = jnp.zeros_like(code)
        for axis in range(3):
            place = (a, b, z)[axis] + shifts[axis]
            low = spans[axis][0]
            if totals[axis] < cells[axis] + 2:
                place = jnp.where(place < 0, place + totals[axis], place)
                place = jnp.where(place >= totals[axis], place - totals[axis], place)
            cell = cell * len(spans[axis]) + (place - low)
        ints_s[2, at, :] = cell
        pairs[c] = (slot, cell, [s.astype(F32) for s in shifts])
        columns_s[c] = jnp.concatenate([slot, jnp.zeros((cap - cand, cap), jnp.int32)], axis=0).T
        for k in range(cand):
            hit = jnp.broadcast_to(columns_s[c, :, k : k + 1], (cap, cap)) == slot_lanes
            onehot[c * cand + k] = jnp.where(hit, 1.0, 0.0).astype(BF16)

    def choose(r, carry):
        where = jnp.broadcast_to(ints_s[2, pl.ds(r, 1), :], (16, cap)) - quarter
        for t in range(tiles):
            chosen[r, 16 * t : 16 * t + 16, :] = jnp.where(where == 4 * t, 1.0, 0.0).astype(BF16)
        return carry

    lax.fori_loop(0, len(inner_cells) * cand, choose, 0)
    w_node_s[...] = w_node_t[:, 0 : 3 * chan].astype(F32).T.astype(BF16)

    w_in_half = (0.5 * w_in[...].astype(F32)).astype(BF16)
    w_in_t = (0.5 * w_in[...].astype(F32)).T.astype(BF16)
    w_out_t = w_out[...].astype(F32).T.astype(BF16)
    diag = lax.broadcasted_iota(jnp.int32, (chan, chan), 0) == lax.broadcasted_iota(jnp.int32, (chan, chan), 1)
    energy_row = jnp.broadcast_to(w_energy[...], (chan, chan))
    energy_col = jnp.sum(jnp.where(diag, energy_row, 0.0), axis=1, keepdims=True)
    kind_rows = lax.broadcasted_iota(jnp.int32, (kinds, cap), 0)
    centres = lax.broadcasted_iota(jnp.int32, (nb, cap), 0).astype(F32) / (nb - 1)
    kind_lanes = lax.broadcasted_iota(jnp.int32, (kinds, cap), 1)
    embed_t[...] = dot(embed[...], (kind_rows == kind_lanes).astype(F32).astype(BF16), 0, 0)
    own_feat = {
        c: dot(embed[...], (kind_rows == rows[c][0]).astype(F32).astype(BF16), 0, 0).astype(BF16)
        for c in rows
    }
    adders = jnp.where(
        lax.broadcasted_iota(jnp.int32, (16, COUNT * 16), 1) // 16
        == lax.broadcasted_iota(jnp.int32, (16, COUNT * 16), 0),
        1.0,
        0.0,
    ).astype(BF16)

    near = {
        c: {
            index_of[tuple(canonical(p + s, n, t) for p, s, n, t in zip(at, move, cells, totals))]
            for move in itertools.product((-1, 0, 1), repeat=3)
        }
        for c, at in enumerate(inner_cells)
    }
    found = {c: [jnp.zeros((cand, cap), F32) for _ in range(4)] for c in near}

    def take(cells_here):
        for e in cells_here:
            for c in near:
                if e in near[c]:
                    slot, cell, _ = pairs[c]
                    hit = cell == e
                    for q in range(4):
                        row = jnp.broadcast_to(table[e, q : q + 1, :], (cand, cap))
                        found[c][q] = jnp.where(hit, jnp.take_along_axis(row, slot, axis=1), found[c][q])

    arriving = {there + j for _, there, _, length in runs for j in range(length)}
    take([i for i in range(len(plan)) if i not in arriving])
    stages = [(z, x) for z in (True, False) for x in (True, False)]
    for stage in stages:
        group = [n for n, r in enumerate(runs) if (r[0][2] == 0, r[0][0] == 0) == stage]
        for n in group:
            copies[n].wait_recv()
        take([runs[n][1] + j for n in group for j in range(runs[n][3])])

    geometry = {}
    for c in near:
        slot, cell, shifts = pairs[c]
        x, y, w = [s + f - m for s, f, m in zip(shifts, found[c], rows[c][3])]
        squared = x * x + y * y + w * w
        rest = jnp.maximum(1.0 - squared, 0.0)
        envelope = rest * rest * rest
        geometry[c] = (x, y, w, squared, rest, envelope)
        at = pl.ds(c * cand, cand)
        rows_s[0, at, :] = squared
        ints_s[0, at, :] = found[c][3].astype(jnp.int32)
        for m, value in enumerate(harmonics(x, y, w)):
            ysc[m, at, :] = envelope if value is None else value * envelope

    sharp = float((nb - 1) ** 2)

    def forward(first, length):
        basis = []
        for k in range(length):
            gap = rows_s[0, pl.ds(first + k, 1), :] - centres
            value = jnp.exp(-sharp * (gap * gap))
            edge_s[first + k] = value * gap
            basis.append(value.astype(BF16))
        half = dot(w_in_t, jnp.concatenate(basis, axis=1))
        half = half.astype(BF16)
        t = jnp.tanh(half)
        up = 1.0 + t
        hidden = half * up
        tilt = up + hidden * (1.0 - t)
        for k in range(length):
            slope[first + k] = tilt[:, k * cap : (k + 1) * cap]
        radial = dot(w_out_t, hidden).astype(BF16)
        weight = []
        for k in range(length):
            row = []
            for m in range(COUNT):
                value = jnp.broadcast_to(ysc[m, pl.ds(first + k, 1), :], (16, cap)).astype(BF16)
                wts[first + k, 16 * m : 16 * m + 16, :] = value
                row.append(value)
            weight.append(row)
        for s in range(chan // 16):
            top = 16 * s
            carried = [[], [], []]
            for k in range(length):
                kind = jnp.broadcast_to(ints_s[0, pl.ds(first + k, 1), :], (16, cap))
                feat = jnp.take_along_axis(embed_t[top : top + 16, :], kind, axis=1).astype(BF16)
                feat_s[first + k, top : top + 16, :] = feat
                for d in range(3):
                    value = radial[d * chan + top : d * chan + top + 16, k * cap : (k + 1) * cap] * feat
                    prod[first + k, d * chan + top : d * chan + top + 16, :] = value
                    carried[d].append(value)
            for base in range(0, length, cand):
                for m in range(COUNT):
                    total = None
                    for low in range(base, base + cand, QUAD):
                        terms = [carried[DEGREE[m]][k] * weight[k][m] for k in range(low, low + QUAD)]
                        while len(terms) > 1:
                            terms = [p + q for p, q in zip(terms[::2], terms[1::2])]
                        part = terms[0].astype(F32)
                        total = part if total is None else total + part
                    msg_s[(first + base) // cand, m, top : top + 16, :] = total

    def node(c):
        occ = rows[c][2]
        msg = [msg_s[c, m] for m in range(COUNT)]
        vector = msg[1] * msg[1] + msg[2] * msg[2] + msg[3] * msg[3]
        tensor = msg[4] * msg[4]
        for m in range(5, 9):
            tensor = tensor + msg[m] * msg[m]
        invariant = jnp.concatenate([msg[0].astype(BF16), vector.astype(BF16), tensor.astype(BF16), own_feat[c]], axis=0)
        active, tilt = silu_parts(dot(w_node_t[...], invariant))
        d_pre = (energy_col * occ * tilt).astype(BF16)
        d_inv = dot(w_node_s[...], d_pre).astype(BF16).astype(F32)
        grad_s[c, 0] = d_inv[0:chan].astype(BF16)
        for m in range(1, COUNT):
            part = d_inv[DEGREE[m] * chan : (DEGREE[m] + 1) * chan]
            grad_s[c, m] = (2.0 * msg[m] * part).astype(BF16)
        return active

    def backward(first, length):
        d_radial = [[[], [], []] for _ in range(length)]
        touched = [[None] * COUNT for _ in range(length)]
        for k in range(length):
            for m in range(COUNT):
                weight = jnp.broadcast_to(ysc[m, pl.ds(first + k, 1), :], (16, cap))
                wts[first + k, 16 * m : 16 * m + 16, :] = weight.astype(BF16)
        for s in range(chan // 16):
            at = slice(16 * s, 16 * s + 16)
            for k in range(length):
                if k % cand == 0:
                    grads = [grad_s[(first + k) // cand, m, at, :] for m in range(COUNT)]
                sums = [None, None, None]
                value = [prod[first + k, d * chan + 16 * s : d * chan + 16 * s + 16, :] for d in range(3)]
                for m in range(COUNT):
                    d = DEGREE[m]
                    term = grads[m] * wts[first + k, 16 * m : 16 * m + 16, :]
                    sums[d] = term if sums[d] is None else sums[d] + term
                    change = value[d] * grads[m]
                    touched[k][m] = change if touched[k][m] is None else touched[k][m] + change
                feat = feat_s[first + k, at, :]
                for d in range(3):
                    d_radial[k][d].append(sums[d] * feat)
        d_radial = [jnp.concatenate([p for q in parts for p in q], axis=0) for parts in d_radial]
        touched = [jnp.concatenate(parts, axis=0) for parts in touched]
        d_hidden = dot(w_out[...], jnp.concatenate(d_radial, axis=1)).astype(BF16)
        d_pre = d_hidden * jnp.concatenate([slope[first + k] for k in range(length)], axis=1)
        d_basis = dot(w_in_half, d_pre).astype(BF16).astype(F32)
        sums = dot(adders, jnp.concatenate(touched, axis=1))
        for k in range(length):
            gsc[pl.ds((first + k) * 16, 16), :] = sums[:, k * cap : (k + 1) * cap]
            piece = d_basis[:, k * cap : (k + 1) * cap] * edge_s[first + k]
            rows_s[1, pl.ds(first + k, 1), :] = jnp.sum(piece, axis=0, keepdims=True)

    sub = lax.broadcasted_iota(jnp.int32, (8, cap), 0) & 3
    forces = {c: [None] * 3 for c in near}

    def finish(c, g):
        at = pl.ds(c * cand + g * 8, 8)
        x, y, w, squared, rest, envelope = [v[g * 8 : g * 8 + 8] for v in geometry[c]]
        grads = [gsc[pl.ds((c * cand + g * 8) * 16 + m, 8, stride=16), :] for m in range(COUNT)]
        d_env = grads[0]
        for m, value in enumerate(harmonics(x, y, w)):
            if m:
                d_env = d_env + value * grads[m]
        d_sq = 2.0 * (-2.0 * sharp * rows_s[1, at, :] - 3.0 * rest * rest * d_env)
        h = [None] + [envelope * grads[m] for m in range(1, 9)]
        gx = x * d_sq + h[1] + SQRT3 * (y * h[4] + w * h[6] + x * h[7]) - x * h[8]
        gy = y * d_sq + h[2] + SQRT3 * (x * h[4] + w * h[5] - y * h[7]) - y * h[8]
        gz = w * d_sq + h[3] + SQRT3 * (y * h[5] + x * h[6]) + 2.0 * w * h[8]
        for d, value in enumerate((gx, gy, gz)):
            rows_s[2 + d, at, :] = value
            forces[c][d] = value if forces[c][d] is None else forces[c][d] + value
        spread = []
        for r in range(c * cand + g * 8, c * cand + g * 8 + 8):
            row = [jnp.broadcast_to(rows_s[2 + d, pl.ds(r, 1), :], (8, cap)) for d in range(3)]
            block = jnp.where(sub == 0, row[0], jnp.where(sub == 1, row[1], row[2]))
            block = jnp.concatenate([block, block], axis=0).astype(BF16)
            spread.append(jnp.concatenate([chosen[r, 16 * t : 16 * t + 16, :] * block for t in range(tiles)], axis=0))
        slots = jnp.concatenate([onehot[r] for r in range(c * cand + g * 8, c * cand + g * 8 + 8)], axis=0)
        return jnp.concatenate(spread, axis=1), slots

    active = {}
    forward(0, len(near) * cand)
    for c in near:
        active[c] = node(c)
    for c in near:
        backward(c * cand, cand)
    pieces = [finish(c, g) for c in near for g in range(cand // 8)]
    scattered = dot(jnp.concatenate([p[0] for p in pieces], axis=1), jnp.concatenate([p[1] for p in pieces], axis=0))
    returns = []
    for n, (step, there, own, length) in enumerate(runs):
        for i in range(there, there + length):
            back[i] = scattered[4 * i : 4 * i + 4]
        copy = pltpu.make_async_remote_copy(
            src_ref=back.at[pl.ds(there, length)],
            dst_ref=landed.at[pl.ds(there, length)],
            send_sem=send_b.at[n],
            recv_sem=recv_b.at[n],
            device_id=device(step),
            device_id_type=MESH,
        )
        copy.start()
        returns.append(copy)
    for i in range(len(plan)):
        if i not in arriving:
            back[i] = scattered[4 * i : 4 * i + 4]
    for c, (a, b, z) in enumerate(inner_cells):
        site_energy[a, b, pl.ds(z, 1), :] = rows[c][2] * jnp.sum(energy_col * active[c], axis=0, keepdims=True)
        forces[c] = [jnp.sum(g, axis=0, keepdims=True) for g in forces[c]]
    totals_here = {}
    for c, at in enumerate(inner_cells):
        gain = rows[c][2] * (0.5 * TIME_STEP) / rows[c][1]
        own = [i for i, (_, _, inner) in enumerate(plan) if inner == at and i not in arriving]
        totals_here[c] = (sum(back[i] for i in own), gain, [rows[c][2] * h for h in rows[c][4]])
    for copy in copies:
        copy.wait_send()
    for copy in returns:
        copy.wait_send()
    for stage in stages:
        group = [n for n, r in enumerate(runs) if (r[0][2] == 0, r[0][0] == 0) == stage]
        for n in group:
            returns[n].wait_recv()
        for c, at in enumerate(inner_cells):
            total, gain, half = totals_here[c]
            for n in group:
                for j in range(runs[n][3]):
                    if plan[runs[n][1] + j][2] == at:
                        total = total + landed[runs[n][1] + j]
            totals_here[c] = (total, gain, half)
    for c, (a, b, z) in enumerate(inner_cells):
        total, gain, half = totals_here[c]
        for d in range(3):
            force = forces[c][d] - total[d : d + 1]
            next_force[d, a, b, pl.ds(z, 1), :] = rows[c][2] * force
            next_velocity[d, a, b, pl.ds(z, 1), :] = half[d] + gain * force


def hand_over(*refs):
    half = len(refs) // 2
    for source, target in zip(refs[:half], refs[half:]):
        target[...] = source[...]


def solution(mesh):
    sizes = tuple(mesh.shape[a] for a in AXES)

    def shards(frac, velocity, force_old, species, cell_count, neighbours, embed, w_in, w_out, w_node, w_energy):
        cells, cap = species.shape[:3], species.shape[3]
        cand, chan, nb = neighbours.shape[0], embed.shape[1], w_in.shape[0]
        _, _, plan = halo_plan(cells, sizes)
        count = cells[0] * cells[1] * cells[2]
        pair_rows = count * cand
        held = len(plan)
        vmem = pl.BlockSpec(memory_space=pltpu.VMEM)
        operands = (frac, velocity, force_old, species, cell_count, neighbours)
        operands += (embed, w_in, w_out, w_node.T, w_energy.reshape(1, -1))
        operands = tuple(pltpu.with_memory_space_constraint(o, pltpu.HBM) for o in operands)
        staged = [pltpu.VMEM(o.shape, o.dtype) for o in operands]
        staged[4] = pltpu.SMEM(cell_count.shape, cell_count.dtype)
        field = jax.ShapeDtypeStruct(frac.shape, F32)
        results = (field, field, field, jax.ShapeDtypeStruct(species.shape, F32))
        outs = pl.pallas_call(
            functools.partial(step_kernel, sizes),
            out_shape=results,
            in_specs=[pl.BlockSpec(memory_space=pl.ANY)] * INPUTS,
            out_specs=(vmem,) * 4,
            scratch_shapes=staged
            + [
                pltpu.VMEM((held, 4, cap), F32),
                pltpu.VMEM((held, 4, cap), F32),
                pltpu.VMEM((held, 4, cap), F32),
                pltpu.VMEM((pair_rows, nb, cap), F32),
                pltpu.VMEM((COUNT, pair_rows, cap), F32),
                pltpu.VMEM((16 * pair_rows, cap), F32),
                pltpu.VMEM((5, pair_rows, cap), F32),
                pltpu.VMEM((3, pair_rows, cap), jnp.int32),
                pltpu.VMEM((count, COUNT, chan, cap), F32),
                pltpu.VMEM((chan, cap), F32),
                pltpu.VMEM((count, cap, cap), jnp.int32),
                pltpu.VMEM((3 * chan, chan), BF16),
                pltpu.SemaphoreType.DMA((held,)),
                pltpu.SemaphoreType.DMA((held,)),
                pltpu.SemaphoreType.DMA((held,)),
                pltpu.SemaphoreType.DMA((held,)),
                pltpu.SemaphoreType.DMA((INPUTS,)),
            ],
            compiler_params=pltpu.CompilerParams(
                collective_id=0, has_side_effects=True, vmem_limit_bytes=32 * 1024 * 1024
            ),
        )(*operands)
        return pl.pallas_call(
            hand_over,
            out_shape=results,
            in_specs=[vmem] * 4,
            out_specs=(vmem,) * 4,
            compiler_params=pltpu.CompilerParams(vmem_limit_bytes=1024 * 1024),
        )(*outs)

    field = P(None, "gx", "gy", "gz", None)
    cell = P("gx", "gy", "gz", None)
    return jax.shard_map(
        shards,
        mesh=mesh,
        in_specs=(field, field, field, cell, P("gx", "gy", "gz"), field, P(), P(), P(), P(), P()),
        out_specs=(field, field, field, cell),
        check_vma=False,
    )
```
